32 devices in a mesh: dp: 2 (over x), row: 4 (over z), col: 4 (over y, core).
Axes of the slice: x: 2, y: 2, z: 4, core: 2. Of those that a mesh axis runs over, the one named last changes fastest.
Arguments:
- tokens: bfloat16 [4096, 768], P(('dp', 'row')), may hold values from -6 to 6
- segments: int32 [8, 512], P(('dp', 'row')), may hold values from 0 to 5, never falling along the last dimension, each value on 1 to 256 neighbouring positions
- routes: int32 [4096, 1], P(('dp', 'row')), may hold values from 0 to 7; in each aligned block of 512 rows (0 to 511, 512 to 1023, ...) at most 128 rows name the same one
- norm_gain: float32 [768], replicated, may hold values from 0.5 to 1.5
- mix_gain: float32 [768], replicated, may hold values from 0.5 to 1.5
- qkv_weight: bfloat16 [768, 3, 768], P('row', None, 'col'), may hold values from -0.21875 to 0.21875
- proj_weight: bfloat16 [768, 768], P('col', 'row'), may hold values from -1.75 to 1.75
- rel_table: float32 [32, 12], P(None, 'col'), may hold values from -95 to 135
- router_weight: float32 [768, 8], replicated, may hold values from -0.109375 to 0.109375
- expert_in: bfloat16 [8, 768, 3072], P(('dp', 'row'), None, 'col'), may hold values from -0.21875 to 0.21875
- expert_out: bfloat16 [8, 3072, 768], P(('dp', 'row'), 'col'), may hold values from -0.875 to 0.875
- cotangent: float32 [4096, 768], P(('dp', 'row')), may hold values from -6 to 6
Outputs:
- output: float32 [4096, 768], P(('dp', 'row'))
- grad_tokens: float32 [4096, 768], P(('dp', 'row'))
- grad_qkv_weight: float32 [768, 3, 768], P('row', None, 'col')
- grad_proj_weight: float32 [768, 768], P('col', 'row')
- grad_rel_table: float32 [32, 12], P(None, 'col')
- grad_norm_gain: float32 [768], replicated
- grad_mix_gain: float32 [768], replicated
- grad_router_weight: float32 [768, 8], replicated
- grad_expert_in: float32 [8, 768, 3072], P(('dp', 'row'), None, 'col')
- grad_expert_out: float32 [8, 3072, 768], P(('dp', 'row'), 'col')
The draws below stay inside these ranges and needn't reach their ends.
Inputs may be any that keep to these rules, and one draw needn't show every extreme that they name: `routes`: in each aligned block of 512 rows (the tokens of one index of dp and row) no expert is named more than 128 times, and in some block one expert is named exactly 128 times. `segments`: along each packed sequence the document numbers never fall; each document covers 1 to 256 positions and one covers exactly 256.
All inputs are finite; a program needn't handle non-finite values.
Results may differ from the reference program's by a relative error of at most 0.012.
The reference program's roundings to bfloat16 on the way count: a program that leaves them out, or rounds other values in their place, can miss the bound.
Values may be sent and summed in bfloat16 or wider, within the bound.
No kernel may reach another device: no remote copies, remote signals or barrier semaphores. Data moves between devices by JAX's collectives and lax.ppermute only.
A program may use at most 128 MiB of HBM per device.

```python
import math
import jax
import jax.numpy as jnp
import numpy as np
from jax import lax

D = 768
HEADS = 12
HEAD_DIM = 64
FF = 3072
BUCKETS = 32
MAX_DIST = 128
LENGTH = 512
SEG_COUNT = 6
HDALL = 768
EXPERTS = 8
TOK_DEV = 512
SEQS = 8
TOKENS = 4096
CAP = 128
SEG_MOST = 256
N_DP = 2
N_ROW = 4


def draw_rel_table(key, part):
    base_draw = jax.random.normal(key, (BUCKETS, HEADS), jnp.float32)
    return base_draw


def shard_levels(rng, extent, cuts, least, largest):
    def one(dim, parts):
        heights = jax.random.uniform(jax.random.fold_in(jax.random.fold_in(rng, 6), dim), (parts,), jnp.float32, least / len(cuts), largest / len(cuts))
        return jnp.repeat(jnp.exp(heights), extent[dim] // parts).reshape((-1,) + (1,) * (len(extent) - dim - 1))

    loudness = one(*cuts[0])
    for cut in cuts[1:]:
        loudness = loudness * one(*cut)
    return loudness


def profile(number_of, total, limit, slope):
    weights = [(1 << 20) // math.isqrt(grade ** slope) + 1 for grade in range(2, number_of + 1)]
    spare, holding = total - limit - (number_of - 1), [1] * (number_of - 1)
    while spare > 0:
        free = [i for i in range(number_of - 1) if holding[i] < limit]
        pool, remaining = sum([weights[i] for i in free]), spare
        for i in free:
            extra = min(limit - holding[i], max(1, remaining * weights[i] // pool), spare)
            holding[i] = holding[i] + extra
            spare = spare - extra
    return np.array([limit] + holding)


def uneven_parts(stream_key, number_of, total, reach, skew):
    if number_of == 2:
        one = jax.random.randint(stream_key, (), max(1, total - reach), min(reach, total - 1) + 1)
        return jnp.stack([one, total - one])
    lengths = jnp.asarray(profile(number_of, total, reach, skew), jnp.int32)
    pairs = (number_of - 1) // 2
    donor, sink = lengths[1:1 + 2 * pairs:2], lengths[2:2 + 2 * pairs:2]
    slack = jnp.minimum(donor - 1, reach - sink)
    moved = jax.random.randint(jax.random.fold_in(stream_key, 1), (pairs,), 0, 1 << 20) % (slack + 1)
    lengths = lengths.at[1:1 + 2 * pairs:2].set(donor - moved).at[2:2 + 2 * pairs:2].set(sink + moved)
    return lengths[jax.random.permutation(jax.random.fold_in(stream_key, 2), number_of)]


def shared_out(own_key, own, number, rows, count, top, bound, slope):
    ranking = jax.random.permutation(own_key, count)
    crowded, common = load_shares(count, rows * top, bound, slope, True), load_shares(count, rows * top, bound, slope, False)
    places = jnp.arange(count)

    def named(sizes, turn):
        used = int((sizes > 0).sum())
        fixed = max(1, used // 4)
        moved = fixed + (places - fixed + turn * (used - fixed)) % max(1, count - fixed)
        return jnp.zeros((count,), jnp.int32).at[ranking[jnp.where(places < fixed, places, moved)]].set(jnp.asarray(sizes, jnp.int32))

    sizes = jnp.where(number % 4 == 0, named(crowded, number // 4), named(common, number - number // 4 - 1))
    mixed = jax.random.permutation(jax.random.fold_in(own, 3), count)
    giver, taker = mixed[0:count // 2 * 2:2], mixed[1:count // 2 * 2:2]
    slack = jnp.minimum(sizes[giver] - 1, bound - sizes[taker]) // 2
    slack = jnp.where((giver == ranking[0]) | (taker == ranking[0]) | (sizes[taker] == 0), 0, jnp.maximum(slack, 0))
    moved = jax.random.randint(jax.random.fold_in(own, 4), (count // 2,), 0, 1 << 20) % (slack + 1)
    sizes = sizes.at[giver].add(-moved).at[taker].add(moved)
    labels = jnp.searchsorted(jnp.cumsum(sizes), jnp.arange(rows * top), side="right").astype(jnp.int32)
    listing = labels.reshape(top, rows).T
    listing = listing[jax.random.permutation(jax.random.fold_in(own, 1), rows)]
    turn = jax.random.randint(jax.random.fold_in(own, 2), (rows, 1), 0, top)
    return jnp.take_along_axis(listing, (jnp.arange(top)[None, :] + turn) % top, axis=1)


def load_shares(number_of, total, limit, lean, full):
    portions = [(1 << 20) // math.isqrt(standing ** lean) + 1 for standing in range(1, number_of + 1)]
    largest = limit if full else min(limit, max(-(-total // number_of), total * portions[0] // sum(portions)))
    least = 1 if total - largest >= number_of - 1 else 0
    counts, surplus = [largest] + [least] * (number_of - 1), total - largest - least * (number_of - 1)
    while surplus > 0:
        movable = [i for i in range(1, number_of) if counts[i] < largest] or [i for i in range(1, number_of) if counts[i] < limit]
        pool, budget = sum([portions[i] for i in movable]), surplus
        for i in movable:
            addition = min(limit - counts[i], max(1, budget * portions[i] // pool), surplus)
            counts[i] = counts[i] + addition
            surplus = surplus - addition
    return np.array(counts)


def gaussian(key, dims, width, reach, split=(), held_as=jnp.bfloat16):
    values = jax.random.normal(key, dims, jnp.float32) * width
    if len(split) > 0:
        values = shard_levels(key, dims, split, -0.22, 0.18) * values
    return jnp.clip(values, min=-reach, max=reach).astype(held_as)


def setup_inputs(seed: int = 0) -> dict:
    key_of = jax.random.split(jax.random.key(seed), 13)
    tokens = gaussian(key_of[0], (TOKENS, D), 1.0, 6.0, ((0, 8),))
    segments = jax.vmap(lambda own: jnp.searchsorted(jnp.cumsum(uneven_parts(own, SEG_COUNT, LENGTH, SEG_MOST, 2)), jnp.arange(LENGTH), side="right"))(jax.random.split(key_of[1], SEQS)).reshape((SEQS, LENGTH)).astype(jnp.int32)
    routes_keys = jax.random.split(jax.random.fold_in(key_of[2], 1), TOKENS // TOK_DEV)
    routes_turns = jax.random.permutation(jax.random.fold_in(key_of[2], 3), TOKENS // TOK_DEV)
    routes = jax.vmap(lambda own, number: shared_out(jax.random.fold_in(key_of[2], 2), own, number, TOK_DEV, EXPERTS, 1, CAP, 1))(routes_keys, routes_turns).reshape((TOKENS, 1))
    norm_gain = jnp.clip(1.0 + 0.1 * jax.random.normal(key_of[3], (D,), jnp.float32), 0.5, 1.5)
    mix_gain = jnp.clip(1.0 + 0.1 * jax.random.normal(key_of[4], (D,), jnp.float32), 0.5, 1.5)
    qkv_weight = gaussian(key_of[5], (D, 3, HDALL), D ** -0.5, 0.21875, ((0, 4), (2, 4)))
    proj_weight = gaussian(key_of[6], (HDALL, D), (HDALL // 64) ** -0.5, 1.75, ((0, 4), (1, 4)))
    rel_table = draw_rel_table(jax.random.fold_in(key_of[12], 71), 0)
    router_weight = gaussian(key_of[8], (D, EXPERTS), (4 * D) ** -0.5, 0.109375, (), jnp.float32)
    expert_in = gaussian(key_of[9], (EXPERTS, D, FF), D ** -0.5, 0.21875, ((0, 8), (2, 4)))
    expert_out = gaussian(key_of[10], (EXPERTS, FF, D), (FF // 64) ** -0.5, 0.875, ((0, 8), (1, 4)))
    cotangent = gaussian(key_of[11], (TOKENS, D), 1.0, 6.0, ((0, 8),), jnp.float32)
    return {"tokens": tokens, "segments": segments, "routes": routes, "norm_gain": norm_gain, "mix_gain": mix_gain, "qkv_weight": qkv_weight, "proj_weight": proj_weight, "rel_table": rel_table, "router_weight": router_weight, "expert_in": expert_in, "expert_out": expert_out, "cotangent": cotangent}


EPS = 1e-06
NEG = -1e+30
GELU_C = 0.7978845608028654
GELU_K = 0.044715

def bucket_edges():
    half_count = BUCKETS // 2
    exact_count = half_count // 2
    edge_list = []
    for target in range(1, half_count):
        if target < exact_count:
            edge_list.append(target)
        else:
            for distance in range(exact_count, MAX_DIST + 1):
                reached = exact_count + int(math.log(distance / exact_count) / math.log(MAX_DIST / exact_count) * (half_count - exact_count))
                if min(reached, half_count - 1) >= target:
                    edge_list.append(distance)
                    break
    return edge_list

def offset_buckets(offsets):
    offsets = offsets.astype(jnp.int32)
    magnitude = jnp.abs(offsets)
    upper = jnp.full(offsets.shape, BUCKETS // 2, jnp.int32)
    result = jnp.where(offsets > 0, upper, jnp.zeros(offsets.shape, jnp.int32))
    for border in bucket_edges():
        result = result + (magnitude >= border).astype(jnp.int32)
    return result.astype(jnp.int32)

def gelu_value(values):
    inner = jnp.tanh(GELU_C * (values + GELU_K * values * values * values))
    return 0.5 * values * (1.0 + inner)

def gelu_slope(values):
    inner = jnp.tanh(GELU_C * (values + GELU_K * values * values * values))
    return 0.5 * (1.0 + inner) + 0.5 * values * (1.0 - inner * inner) * GELU_C * (1.0 + 3.0 * GELU_K * values * values)

def through_bf16(values):
    return lax.optimization_barrier(values.astype(jnp.bfloat16)).astype(jnp.float32)

def norm_rows(values, weights):
    inverse = lax.rsqrt(lax.optimization_barrier(jnp.mean(values * values, axis=-1, keepdims=True)) + EPS)
    return (values * inverse * weights, inverse)

def norm_back(values, weights, inverse, grad_normed):
    row_width = values.shape[-1]
    inner_sum = lax.optimization_barrier(jnp.sum(grad_normed * weights * values, axis=-1, keepdims=True))
    grad_values = inverse * weights * grad_normed - values * inverse ** 3 * inner_sum / row_width
    grad_weights = lax.optimization_barrier(jnp.sum(grad_normed * values * inverse, axis=0))
    return (grad_values, grad_weights)

def position_bias(rel_table):
    positions = jnp.arange(LENGTH, dtype=jnp.int32)
    bucket_ids = offset_buckets(positions[None, :] - positions[:, None])
    bucket_hot = (bucket_ids[:, :, None] == jnp.arange(BUCKETS, dtype=jnp.int32)[None, None, :]).astype(jnp.float32)
    pos_bias = jnp.einsum('ijb,bh->hij', bucket_hot, rel_table, precision=lax.Precision.HIGHEST)
    return (pos_bias, bucket_hot)

def masked_scores(queries, key_rows, seg_row, pos_bias):
    scores = jnp.einsum('ihd,jhd->hij', queries, key_rows) * HEAD_DIM ** (-0.5) + pos_bias
    same_doc = seg_row[:, None] == seg_row[None, :]
    return jnp.where(same_doc[None], scores, jnp.asarray(NEG, scores.dtype))

def split_heads(qkv_seq):
    heads_all = qkv_seq.reshape(LENGTH, 3, HEADS, HEAD_DIM).astype(jnp.float32)
    return (heads_all[:, 0], heads_all[:, 1], heads_all[:, 2])

def attend_forward(packed, pos_bias):
    qkv_seq, seg_row = packed
    queries, key_rows, values = split_heads(qkv_seq)
    scores = masked_scores(queries, key_rows, seg_row, pos_bias)
    row_max = lax.optimization_barrier(jnp.max(scores, axis=-1, keepdims=True))
    exponent = jnp.exp(scores - row_max)
    row_total = lax.optimization_barrier(jnp.sum(exponent, axis=-1, keepdims=True))
    attn_probs = exponent / row_total
    log_total = row_max + jnp.log(row_total)
    weights_bf = through_bf16(attn_probs)
    attended = jnp.einsum('hij,jhd->ihd', weights_bf, values).astype(jnp.bfloat16)
    return (attended.reshape(LENGTH, HEADS * HEAD_DIM), log_total)

def attend_backward(packed, pos_bias, bucket_hot):
    qkv_seq, seg_row, log_total, attended, grad_seq = packed
    queries, key_rows, values = split_heads(qkv_seq)
    scores = masked_scores(queries, key_rows, seg_row, pos_bias)
    attn_probs = jnp.exp(scores - log_total)
    weights_bf = through_bf16(attn_probs)
    grad_heads = grad_seq.reshape(LENGTH, HEADS, HEAD_DIM).astype(jnp.float32)
    out_heads = attended.reshape(LENGTH, HEADS, HEAD_DIM).astype(jnp.float32)
    row_delta = lax.optimization_barrier(jnp.sum(grad_heads * out_heads, axis=-1))
    grad_probs = jnp.einsum('ihd,jhd->hij', grad_heads, values)
    grad_scores = attn_probs * (grad_probs - row_delta.T[:, :, None])
    grad_bf = through_bf16(grad_scores)
    scale_value = HEAD_DIM ** (-0.5)
    grad_query = (jnp.einsum('hij,jhd->ihd', grad_bf, key_rows) * scale_value).astype(jnp.bfloat16)
    grad_key = (jnp.einsum('hij,ihd->jhd', grad_bf, queries) * scale_value).astype(jnp.bfloat16)
    grad_value = jnp.einsum('hij,ihd->jhd', weights_bf, grad_heads).astype(jnp.bfloat16)
    grad_qkv = jnp.stack([grad_query, grad_key, grad_value], axis=1).reshape(LENGTH, 3, HEADS * HEAD_DIM)
    grad_table = jnp.einsum('hij,ijb->bh', grad_scores, bucket_hot, precision=lax.Precision.HIGHEST)
    return (grad_qkv, grad_table)

def slot_places(chosen):
    blocks = chosen.reshape(-1, TOK_DEV)
    expert_hits = (blocks[:, :, None] == jnp.arange(EXPERTS, dtype=jnp.int32)[None, None, :]).astype(jnp.int32)
    earlier = jnp.cumsum(expert_hits, axis=1, dtype=jnp.int32) - expert_hits
    slot_rank = lax.optimization_barrier(jnp.sum(earlier * expert_hits, axis=-1, dtype=jnp.int32))
    sources = jnp.arange(blocks.shape[0], dtype=jnp.int32)[:, None]
    return (sources * CAP + slot_rank).reshape(-1).astype(jnp.int32)

def expert_forward(packed):
    slot_rows, weight_in, weight_out = packed
    pre_act = jnp.dot(slot_rows, weight_in, preferred_element_type=jnp.float32)
    activation = gelu_value(pre_act).astype(jnp.bfloat16)
    return jnp.dot(activation, weight_out, preferred_element_type=jnp.float32).astype(jnp.bfloat16)

def expert_backward(packed):
    slot_rows, grad_rows, weight_in, weight_out = packed
    pre_act = jnp.dot(slot_rows, weight_in, preferred_element_type=jnp.float32)
    activation = gelu_value(pre_act).astype(jnp.bfloat16)
    grad_act = jnp.dot(grad_rows, weight_out.T, preferred_element_type=jnp.float32)
    grad_pre = (grad_act * gelu_slope(pre_act)).astype(jnp.bfloat16)
    grad_out_w = jnp.dot(activation.T, grad_rows, preferred_element_type=jnp.float32)
    grad_in_w = jnp.dot(slot_rows.T, grad_pre, preferred_element_type=jnp.float32)
    grad_slots = jnp.dot(grad_pre, weight_in.T, preferred_element_type=jnp.float32)
    return (grad_in_w, grad_out_w, grad_slots)

def reference(tokens, segments, routes, norm_gain, mix_gain, qkv_weight, proj_weight, rel_table, router_weight, expert_in, expert_out, cotangent):
    inputs = tokens.astype(jnp.float32)
    normed_one, inverse_one = norm_rows(inputs, norm_gain)
    normed_bf = normed_one.astype(jnp.bfloat16)
    qkv_matrix = qkv_weight.reshape(D, 3 * HDALL)
    qkv_rows = jnp.dot(normed_bf, qkv_matrix, preferred_element_type=jnp.float32).astype(jnp.bfloat16)
    qkv_seqs = qkv_rows.reshape(SEQS, LENGTH, 3, HDALL)
    pos_bias, bucket_hot = position_bias(rel_table)
    attended, log_totals = lax.map(lambda packed: attend_forward(packed, pos_bias), (qkv_seqs, segments))
    attended_rows = attended.reshape(TOKENS, HDALL)
    hidden = inputs + jnp.dot(attended_rows, proj_weight, preferred_element_type=jnp.float32)
    normed_two, inverse_two = norm_rows(hidden, mix_gain)
    logits = jnp.dot(normed_two, router_weight, precision=lax.Precision.HIGHEST, preferred_element_type=jnp.float32)
    router_probs = jax.nn.softmax(logits, axis=-1)
    chosen = routes[:, 0].astype(jnp.int32)
    picked = (chosen[:, None] == jnp.arange(EXPERTS, dtype=jnp.int32)[None, :]).astype(jnp.float32)
    gate_prob = lax.optimization_barrier(jnp.sum(router_probs * picked, axis=-1))
    expert_tokens = normed_two.astype(jnp.bfloat16)
    slot_index = slot_places(chosen)
    slot_total = N_DP * N_ROW * CAP
    token_buffer = jnp.zeros((EXPERTS, slot_total, D), jnp.bfloat16).at[chosen, slot_index].set(expert_tokens)
    expert_result = lax.map(expert_forward, (token_buffer, expert_in, expert_out))
    mixed_rows = lax.optimization_barrier(expert_result[chosen, slot_index]).astype(jnp.float32)
    output = hidden + gate_prob[:, None] * mixed_rows
    grad_gate = lax.optimization_barrier(jnp.sum(cotangent * mixed_rows, axis=-1))
    grad_mixed = (gate_prob[:, None] * cotangent).astype(jnp.bfloat16)
    grad_buffer = jnp.zeros((EXPERTS, slot_total, D), jnp.bfloat16).at[chosen, slot_index].set(grad_mixed)
    grad_expert_in, grad_expert_out, grad_slot_rows = lax.map(expert_backward, (token_buffer, grad_buffer, expert_in, expert_out))
    grad_from_expert = grad_slot_rows[chosen, slot_index]
    grad_logits = grad_gate[:, None] * gate_prob[:, None] * (picked - router_probs)
    grad_router_weight = jnp.dot(normed_two.T, grad_logits, precision=lax.Precision.HIGHEST, preferred_element_type=jnp.float32)
    grad_normed_two = grad_from_expert + jnp.dot(grad_logits, router_weight.T, precision=lax.Precision.HIGHEST, preferred_element_type=jnp.float32)
    grad_hidden_norm, grad_mix_gain = norm_back(hidden, mix_gain, inverse_two, grad_normed_two)
    grad_hidden = cotangent + grad_hidden_norm
    grad_hidden_bf = grad_hidden.astype(jnp.bfloat16)
    grad_proj_weight = jnp.dot(attended_rows.T, grad_hidden_bf, preferred_element_type=jnp.float32)
    grad_attended = jnp.dot(grad_hidden_bf, proj_weight.T, preferred_element_type=jnp.float32).astype(jnp.bfloat16)
    grad_qkv_seqs, grad_table_seqs = lax.map(lambda packed: attend_backward(packed, pos_bias, bucket_hot), (qkv_seqs, segments, log_totals, attended, grad_attended.reshape(SEQS, LENGTH, HDALL)))
    grad_rel_table = lax.optimization_barrier(jnp.sum(grad_table_seqs, axis=0))
    grad_qkv_rows = grad_qkv_seqs.reshape(TOKENS, 3 * HDALL)
    grad_qkv_weight = jnp.dot(normed_bf.T, grad_qkv_rows, preferred_element_type=jnp.float32).reshape(D, 3, HDALL)
    grad_normed_one = jnp.dot(grad_qkv_rows, qkv_matrix.T, preferred_element_type=jnp.float32)
    grad_input_norm, grad_norm_gain = norm_back(inputs, norm_gain, inverse_one, grad_normed_one)
    grad_tokens = grad_hidden + grad_input_norm
    return (output, grad_tokens, grad_qkv_weight, grad_proj_weight, grad_rel_table, grad_norm_gain, grad_mix_gain, grad_router_weight, grad_expert_in, grad_expert_out)
```

```python
import math

import jax
import jax.numpy as jnp
from jax import lax
from jax.experimental import pallas as pl
from jax.experimental.pallas import tpu as pltpu
from jax.sharding import PartitionSpec as P

BUCKETS = 32
MAX_DIST = 128
EPS = 1e-06
NEG = -1e30
GELU_C = 0.7978845608028654
GELU_K = 0.044715
BF = jnp.bfloat16
F32 = jnp.float32
HI = lax.Precision.HIGHEST
DR = ("dp", "row")


def bucket_edges():
    half_count = BUCKETS // 2
    exact_count = half_count // 2
    edge_list = []
    for target in range(1, half_count):
        if target < exact_count:
            edge_list.append(target)
        else:
            for distance in range(exact_count, MAX_DIST + 1):
                reached = exact_count + int(
                    math.log(distance / exact_count)
                    / math.log(MAX_DIST / exact_count)
                    * (half_count - exact_count)
                )
                if min(reached, half_count - 1) >= target:
                    edge_list.append(distance)
                    break
    return edge_list


def offset_onehot(length):
    offsets = jnp.arange(2 * length, dtype=jnp.int32) - (length - 1)
    magnitude = jnp.abs(offsets)
    ids = jnp.where(offsets > 0, BUCKETS // 2, 0)
    for border in bucket_edges():
        ids = ids + (magnitude >= border).astype(jnp.int32)
    ids = jnp.where(offsets >= length, -1, ids)
    return (ids[:, None] == jnp.arange(BUCKETS, dtype=jnp.int32)[None, :]).astype(F32)


def bias_kernel(off_ref, out_ref):
    heads, length, _ = out_ref.shape
    for h in range(heads):
        rows = jnp.broadcast_to(off_ref[h : h + 1, :], (length, 2 * length))
        skewed = pltpu.roll(rows, 1, 1, stride=1, stride_axis=0)
        out_ref[h] = skewed[:, length:]


def position_bias(per_offset, length):
    heads = per_offset.shape[0]
    return pl.pallas_call(
        bias_kernel,
        out_shape=jax.ShapeDtypeStruct((heads, length, length), F32),
        name="position_bias",
        cost_estimate=pl.CostEstimate(
            flops=heads * length * length * 4, bytes_accessed=heads * length * length * 4, transcendentals=0
        ),
    )(per_offset)


def head_parts(qkv_ref, h, heads, size):
    width = heads * size
    return tuple(qkv_ref[:, part * width + h * size : part * width + (h + 1) * size] for part in range(3))


def dot_t(a, b):
    return lax.dot_general(a, b, (((1,), (1,)), ((), ())), preferred_element_type=F32)


def t_dot(a, b):
    return lax.dot_general(a, b, (((0,), (0,)), ((), ())), preferred_element_type=F32)


def attend_kernel(qkv_ref, seg_row_ref, seg_col_ref, bias_ref, out_ref, lse_ref):
    heads = bias_ref.shape[0]
    size = out_ref.shape[1] // heads
    same = seg_col_ref[...] == seg_row_ref[...]
    for h in range(heads):
        q, k, v = head_parts(qkv_ref, h, heads, size)
        scores = dot_t(q, k) * size ** (-0.5) + bias_ref[h]
        scores = jnp.where(same, scores, NEG)
        top = jnp.max(scores, axis=1, keepdims=True)
        expo = jnp.exp(scores - top)
        total = jnp.sum(expo, axis=1, keepdims=True)
        probs = (expo * (1.0 / total)).astype(BF)
        out_ref[:, h * size : (h + 1) * size] = jnp.dot(probs, v, preferred_element_type=F32).astype(BF)
        lse_ref[h] = top + jnp.log(total)


def attend(qkv, seg_row, seg_col, bias):
    length = qkv.shape[0]
    heads = bias.shape[0]
    width = qkv.shape[1] // 3
    return pl.pallas_call(
        attend_kernel,
        out_shape=(
            jax.ShapeDtypeStruct((length, width), BF),
            jax.ShapeDtypeStruct((heads, length, 1), F32),
        ),
        name="attend",
        cost_estimate=pl.CostEstimate(
            flops=4 * length * length * width, bytes_accessed=heads * length * length * 4,
            transcendentals=heads * length * length,
        ),
    )(qkv, seg_row, seg_col, bias)


def attend_back_kernel(qkv_ref, seg_row_ref, seg_col_ref, bias_ref, lse_ref, out_ref, grad_ref, gqkv_ref, off_ref):
    heads, length, _ = bias_ref.shape
    size = out_ref.shape[1] // heads
    width = heads * size
    scale = size ** (-0.5)
    same = seg_col_ref[...] == seg_row_ref[...]
    for h in range(heads):
        q, k, v = head_parts(qkv_ref, h, heads, size)
        cols = slice(h * size, (h + 1) * size)
        scores = dot_t(q, k) * scale + bias_ref[h]
        scores = jnp.where(same, scores, NEG)
        probs = jnp.exp(scores - lse_ref[h])
        grad_out = grad_ref[:, cols]
        delta = jnp.sum(grad_out.astype(F32) * out_ref[:, cols].astype(F32), axis=1, keepdims=True)
        grad_scores = probs * (dot_t(grad_out, v) - delta)
        grad_bf = grad_scores.astype(BF)
        gqkv_ref[:, h * size : (h + 1) * size] = (jnp.dot(grad_bf, k, preferred_element_type=F32) * scale).astype(BF)
        gqkv_ref[:, width + h * size : width + (h + 1) * size] = (t_dot(grad_bf, q) * scale).astype(BF)
        gqkv_ref[:, 2 * width + h * size : 2 * width + (h + 1) * size] = t_dot(probs.astype(BF), grad_out).astype(BF)
        rows = jnp.concatenate([jnp.zeros_like(grad_scores), grad_scores], axis=1)
        count = length // 2
        while count >= 8:
            rows = rows[:count] + pltpu.roll(rows[count:], 2 * length - count, 1)
            count //= 2
        off_ref[h] = rows


def attend_back(qkv, seg_row, seg_col, bias, lse, attended, grad_attended):
    length = qkv.shape[0]
    heads = bias.shape[0]
    width = qkv.shape[1] // 3
    return pl.pallas_call(
        attend_back_kernel,
        out_shape=(
            jax.ShapeDtypeStruct((length, 3 * width), BF),
            jax.ShapeDtypeStruct((heads, 8, 2 * length), F32),
        ),
        name="attend_back",
        cost_estimate=pl.CostEstimate(
            flops=10 * length * length * width, bytes_accessed=heads * length * length * 4,
            transcendentals=heads * length * length,
        ),
    )(qkv, seg_row, seg_col, bias, lse, attended, grad_attended)


def swap(x, axes, count, mask):
    return lax.ppermute(x, axes, [(i, i ^ mask) for i in range(count)])


def bits_of(count):
    return [1 << b for b in range(count.bit_length() - 1)]


def gather_rel(x, axes, count):
    blocks = {0: x}
    for bit in reversed(bits_of(count)):
        blocks.update({k | bit: swap(v, axes, count, bit) for k, v in blocks.items()})
    return [blocks[k] for k in range(count)]


def scatter_rel(blocks, axes, count):
    held = dict(enumerate(blocks))
    for bit in bits_of(count):
        got = {k: swap(held[k | bit].astype(BF), axes, count, bit) for k in held if not k & bit}
        held = {k: held[k].astype(F32) + got[k].astype(F32) for k in got}
    return held[0]


def exchange_rel(blocks, axes, count):
    return [blocks[0]] + [swap(blocks[k], axes, count, k) for k in range(1, count)]


def hold(x, *after):
    return lax.optimization_barrier((x,) + after)[0]


def in_order(blocks, index):
    count = len(blocks)
    if count == 2:
        first = jnp.where(index == 0, blocks[0], blocks[1])
        second = jnp.where(index == 0, blocks[1], blocks[0])
        return jnp.concatenate([first, second], axis=0)
    stacked = jnp.stack(blocks)
    return jnp.concatenate(
        [lax.dynamic_index_in_dim(stacked, index ^ j, 0, keepdims=False) for j in range(count)], axis=0
    )


def on_device(
    tokens,
    segments,
    routes,
    norm_gain,
    mix_gain,
    qkv_weight,
    proj_weight,
    rel_table,
    router_weight,
    expert_in,
    expert_out,
    cotangent,
):
    n_dp, n_row, n_col = lax.axis_size("dp"), lax.axis_size("row"), lax.axis_size("col")
    experts = n_dp * n_row
    dp, row, col = lax.axis_index("dp"), lax.axis_index("row"), lax.axis_index("col")
    me = dp * n_row + row
    count, width = tokens.shape
    length = segments.shape[1]
    heads = rel_table.shape[1]
    local = proj_weight.shape[0]
    block = width // n_row
    own = count // n_col
    slots = 2 * count // experts // n_col
    total_slots = experts * slots
    w_in, w_out = expert_in[0], expert_out[0]

    qkv_own = qkv_weight.reshape(block, 3 * local)
    qkv_rel = jnp.concatenate(
        [qkv_own] + [swap(qkv_own, "row", n_row, k) for k in range(1, n_row)], axis=0
    )
    proj_after = hold(proj_weight, qkv_rel)
    proj_rel_cols = jnp.concatenate(
        [proj_weight] + [swap(proj_after, "row", n_row, k) for k in range(1, n_row)], axis=1
    )

    feature = jnp.arange(width, dtype=jnp.int32)
    part = block // n_dp
    to_rel = ((feature // block) ^ row) * block + feature % block
    to_rel2 = ((feature // block) ^ row) * block + ((feature % block // part) ^ dp) * part + feature % part
    perm_rel = (feature[:, None] == to_rel[None, :]).astype(BF)
    perm_rel2 = (feature[:, None] == to_rel2[None, :]).astype(BF)

    chosen = routes[:, 0]
    expert_ids = jnp.arange(experts, dtype=jnp.int32)
    hits = (expert_ids[:, None] == chosen[None, :]).astype(F32)
    place = jnp.arange(count, dtype=jnp.int32)
    before = (place[:, None] < place[None, :]).astype(BF)
    earlier = jnp.dot(hits.astype(BF), before, preferred_element_type=F32)
    totals = jnp.sum(hits, axis=1)
    starts = jnp.sum(
        jnp.where(expert_ids[None, :] < expert_ids[:, None], totals[None, :], 0.0), axis=1
    )
    start = jnp.sum(hits * starts[:, None], axis=0).astype(jnp.int32)
    rank = jnp.sum(hits * earlier, axis=0).astype(jnp.int32)
    spot = start + rank
    owner, inner = spot % n_col, spot // n_col
    dest = (owner ^ col) * own + inner
    perm = (place[:, None] == dest[None, :]).astype(BF)
    perm_own = perm[:own]
    local_rank = inner - (start + n_col - 1 - col) // n_col
    slot = jnp.where(owner == col, (chosen ^ me) * slots + local_rank, -1)
    slot_ids = jnp.arange(total_slots, dtype=jnp.int32)
    slot_of_token = (slot_ids[:, None] == slot[None, :]).astype(BF)
    slot_of_own = dot_t(slot_of_token, perm_own).astype(BF)
    picked = dot_t(perm_own, hits.astype(BF))

    inputs = tokens.astype(F32)
    inverse = lax.rsqrt(jnp.mean(inputs * inputs, axis=1, keepdims=True) + EPS)
    normed_bf = (inputs * inverse * norm_gain).astype(BF)
    normed_rel = jnp.dot(normed_bf, perm_rel, preferred_element_type=F32).astype(BF)
    normed_rel2 = jnp.dot(normed_bf, perm_rel2, preferred_element_type=F32).astype(BF)
    tokens_perm = jnp.dot(perm, tokens, preferred_element_type=F32)
    inverse_perm = lax.rsqrt(jnp.mean(tokens_perm * tokens_perm, axis=1, keepdims=True) + EPS)
    tokens_own, inverse_own = tokens_perm[:own], inverse_perm[:own]
    cot_own = jnp.dot(perm_own.astype(F32), cotangent, precision=HI, preferred_element_type=F32)

    onehot = offset_onehot(length)
    per_offset = jnp.dot(rel_table.T, onehot.T, precision=HI, preferred_element_type=F32)
    bias = position_bias(per_offset, length)

    cot_slots = jnp.dot(slot_of_token, cotangent.astype(BF), preferred_element_type=F32).astype(BF)
    cot_slots = hold(cot_slots, qkv_rel)
    cot_came = exchange_rel(
        [cot_slots[k * slots : (k + 1) * slots] for k in range(experts)], DR, experts
    )
    cot_blocks = gather_rel(jnp.concatenate(cot_came, axis=0), "col", n_col)
    raw_blocks = [dot_t(b, w_out) for b in cot_blocks]

    qkv_rows = jnp.dot(normed_rel, qkv_rel, preferred_element_type=F32).astype(BF)
    seg_row, seg_col = segments.reshape(1, length), segments.reshape(length, 1)
    attended, lse = attend(qkv_rows, seg_row, seg_col, bias)
    attended_perm = jnp.dot(perm, attended, preferred_element_type=F32).astype(BF)
    attended_own = jnp.concatenate(
        exchange_rel([attended_perm[k * own : (k + 1) * own] for k in range(n_col)], "col", n_col),
        axis=1,
    )
    proj_local = dot_t(proj_rel_cols, perm_rel).astype(BF)
    proj_full = jnp.concatenate(gather_rel(proj_local, "col", n_col), axis=0)
    attn_out = jnp.dot(attended_own, proj_full, preferred_element_type=F32)
    hidden = tokens_own + attn_out

    inverse_two = lax.rsqrt(jnp.mean(hidden * hidden, axis=1, keepdims=True) + EPS)
    normed_two = hidden * inverse_two * mix_gain
    logits = jnp.dot(normed_two, router_weight, precision=HI, preferred_element_type=F32)
    router_probs = jax.nn.softmax(logits, axis=-1)
    gate = jnp.sum(router_probs * picked, axis=1, keepdims=True)
    gate_hi = gate.astype(BF)
    gate_lo = (gate - gate_hi.astype(F32)).astype(BF)
    payload = jnp.concatenate(
        [normed_two.astype(BF), gate_hi, gate_lo, jnp.zeros((own, 126), BF)], axis=1
    )
    token_slots = jnp.dot(slot_of_own, payload, preferred_element_type=F32).astype(BF)
    token_came = exchange_rel(
        [token_slots[k * slots : (k + 1) * slots] for k in range(experts)], DR, experts
    )
    token_blocks = gather_rel(jnp.concatenate(token_came, axis=0), "col", n_col)

    acts, pres, mixed_parts, back_parts, gated = [], [], [], [], []
    for block_rows, raw, cot_rows in zip(token_blocks, raw_blocks, cot_blocks):
        rows = block_rows[:, :width]
        slot_gate = block_rows[:, width : width + 1].astype(F32) + block_rows[:, width + 1 : width + 2].astype(F32)
        pre = jnp.dot(rows, w_in, preferred_element_type=F32)
        inner_t = jnp.tanh(GELU_C * (pre + GELU_K * pre * pre * pre))
        act = (0.5 * pre * (1.0 + inner_t)).astype(BF)
        slope = 0.5 * (1.0 + inner_t) + 0.5 * pre * (1.0 - inner_t * inner_t) * GELU_C * (
            1.0 + 3.0 * GELU_K * pre * pre
        )
        grad_pre = (slot_gate * raw * slope).astype(BF)
        mixed_parts.append(jnp.dot(act, w_out, preferred_element_type=F32))
        back_parts.append(dot_t(grad_pre, w_in))
        acts.append(act)
        pres.append(grad_pre)
        gated.append((slot_gate * cot_rows.astype(F32)).astype(BF))
    def to_home(parts):
        summed = scatter_rel(parts, "col", n_col).astype(BF)
        returned = exchange_rel([summed[k * slots : (k + 1) * slots] for k in range(experts)], DR, experts)
        return t_dot(slot_of_own, jnp.concatenate(returned, axis=0))
    mixed = to_home(mixed_parts)
    grad_from_expert = to_home(back_parts)
    rows_all = jnp.concatenate([b[:, :width] for b in token_blocks], axis=0)
    grad_in_local = t_dot(rows_all, jnp.concatenate(pres, axis=0))
    grad_out_local = t_dot(jnp.concatenate(acts, axis=0), jnp.concatenate(gated, axis=0))

    grad_gate = jnp.sum(cot_own * mixed, axis=1, keepdims=True)
    grad_logits = grad_gate * gate * (picked - router_probs)
    router_local = lax.dot_general(
        normed_two, grad_logits, (((0,), (0,)), ((), ())), precision=HI, preferred_element_type=F32
    )
    grad_normed_two = grad_from_expert + lax.dot_general(
        grad_logits, router_weight, (((1,), (1,)), ((), ())), precision=HI, preferred_element_type=F32
    )
    mix_local = jnp.sum(grad_normed_two * hidden * inverse_two, axis=0)
    inner_two = jnp.sum(grad_normed_two * mix_gain * hidden, axis=1, keepdims=True)
    grad_hidden = (
        cot_own
        + inverse_two * mix_gain * grad_normed_two
        - hidden * inverse_two**3 * inner_two / width
    )
    grad_hidden_perm = jnp.concatenate(gather_rel(grad_hidden.astype(BF), "col", n_col), axis=0)
    grad_attended_perm = dot_t(grad_hidden_perm, proj_local).astype(BF)
    grad_attended = t_dot(perm, grad_attended_perm).astype(BF)
    out_delta = (attn_out + gate * mixed).astype(BF)
    out_delta = hold(out_delta, grad_hidden_perm)
    out_perm = jnp.concatenate(gather_rel(out_delta, "col", n_col), axis=0)
    output = inputs + t_dot(perm, out_perm)

    grad_hidden_rel = jnp.dot(grad_hidden_perm, perm_rel2, preferred_element_type=F32).astype(BF)
    proj_grad = t_dot(grad_hidden_rel, attended_perm)

    def reduce_weight(grad):
        parts = grad.astype(BF).reshape(n_row, n_dp, part, grad.shape[1])
        summed = grad.reshape(parts.shape)[0, 0]
        for k in range(n_row):
            for q in range(n_dp):
                if k or q:
                    summed = summed + swap(parts[k, q], DR, experts, q * n_row + k).astype(F32)
        shared = gather_rel(summed.astype(BF), "dp", n_dp)
        return in_order(shared, dp).astype(F32)

    grad_proj = reduce_weight(proj_grad).T

    grad_qkv, off_sums = attend_back(
        qkv_rows, seg_row, seg_col, bias, lse, attended, grad_attended
    )
    qkv_grad = t_dot(normed_rel2, grad_qkv)
    grad_qkv_weight = reduce_weight(qkv_grad).reshape(block, 3, local)
    grad_qkv_perm = jnp.dot(perm, grad_qkv, preferred_element_type=F32).astype(BF)
    qkv_abs = jnp.dot(perm_rel, qkv_rel, preferred_element_type=F32).astype(BF)
    normed_part = dot_t(grad_qkv_perm, qkv_abs)
    norm_local = jnp.sum(normed_part * tokens_perm * inverse_perm, axis=0)
    grad_normed_one = scatter_rel(
        [normed_part[k * own : (k + 1) * own] for k in range(n_col)], "col", n_col
    )
    inner_one = jnp.sum(grad_normed_one * norm_gain * tokens_own, axis=1, keepdims=True)
    tokens_delta = (
        (grad_hidden - cot_own)
        + inverse_own * norm_gain * grad_normed_one
        - tokens_own * inverse_own**3 * inner_one / width
    )
    tokens_delta_perm = jnp.concatenate(
        gather_rel(tokens_delta.astype(BF), "col", n_col), axis=0
    )
    grad_tokens = cotangent + t_dot(perm, tokens_delta_perm)

    off_sums = jnp.pad(off_sums, ((0, 0), (0, 0), (0, 8)))
    off_total = sum(off_sums[:, i, 1 + i : 1 + i + 2 * length] for i in range(8))
    table_local = jnp.dot(off_total, onehot, precision=HI, preferred_element_type=F32)
    sizes = [width, width, width * experts, heads * BUCKETS]
    flat = jnp.concatenate(
        [norm_local, mix_local, router_local.reshape(-1), table_local.reshape(-1)]
    )
    flat = jnp.pad(flat, (0, -flat.size % 1024)).reshape(-1, 128)
    for bit in bits_of(experts):
        flat = flat + swap(flat, DR, experts, bit)
    grad_table = flat.reshape(-1)[sum(sizes[:3]) : sum(sizes)].reshape(heads, BUCKETS).T
    for bit in bits_of(n_col):
        flat = flat + swap(flat, "col", n_col, bit)
    flat = flat.reshape(-1)
    grad_norm = flat[:width]
    grad_mix = flat[width : 2 * width]
    grad_router = flat[2 * width : 2 * width + sizes[2]].reshape(width, experts)
    return (
        output,
        grad_tokens,
        grad_qkv_weight,
        grad_proj,
        grad_table,
        grad_norm,
        grad_mix,
        grad_router,
        grad_in_local[None],
        grad_out_local[None],
    )


def solution(mesh):
    placed = (
        P(("dp", "row"), None),
        P(("dp", "row"), None),
        P(("dp", "row"), None),
        P(),
        P(),
        P("row", None, "col"),
        P("col", "row"),
        P(None, "col"),
        P(),
        P(("dp", "row"), None, "col"),
        P(("dp", "row"), "col", None),
        P(("dp", "row"), None),
    )
    return jax.shard_map(
        on_device,
        mesh=mesh,
        in_specs=placed,
        out_specs=(
            P(("dp", "row"), None),
            P(("dp", "row"), None),
            P("row", None, "col"),
            P("col", "row"),
            P(None, "col"),
            P(),
            P(),
            P(),
            P(("dp", "row"), None, "col"),
            P(("dp", "row"), "col", None),
        ),
        check_vma=False,
    )
```

```python
from functools import partial
import math

import jax
import jax.numpy as jnp
from jax import lax
from jax.experimental import pallas as pl
from jax.experimental.pallas import tpu as pltpu
from jax.sharding import PartitionSpec as P

BUCKETS = 32
MAX_DIST = 128
EPS = 1e-06
NEG = -1e30
GELU_C = 0.7978845608028654
GELU_K = 0.044715
BF = jnp.bfloat16
F32 = jnp.float32
HI = lax.Precision.HIGHEST
DR = ("dp", "row")


def bucket_edges():
    half_count = BUCKETS // 2
    exact_count = half_count // 2
    edge_list = []
    for target in range(1, half_count):
        if target < exact_count:
            edge_list.append(target)
        else:
            for distance in range(exact_count, MAX_DIST + 1):
                reached = exact_count + int(
                    math.log(distance / exact_count)
                    / math.log(MAX_DIST / exact_count)
                    * (half_count - exact_count)
                )
                if min(reached, half_count - 1) >= target:
                    edge_list.append(distance)
                    break
    return edge_list


def offset_onehot(length):
    offsets = jnp.arange(2 * length, dtype=jnp.int32) - (length - 1)
    magnitude = jnp.abs(offsets)
    ids = jnp.where(offsets > 0, BUCKETS // 2, 0)
    for border in bucket_edges():
        ids = ids + (magnitude >= border).astype(jnp.int32)
    ids = jnp.where(offsets >= length, -1, ids)
    return (ids[:, None] == jnp.arange(128, dtype=jnp.int32)[None, :]).astype(F32)


def bias_kernel(off_ref, out_ref):
    heads, length, _ = out_ref.shape
    for h in range(heads):
        rows = jnp.broadcast_to(off_ref[h : h + 1, :], (length, 2 * length))
        skewed = pltpu.roll(rows, 1, 1, stride=1, stride_axis=0)
        out_ref[h] = skewed[:, length:]


def position_bias(per_offset, length):
    heads = per_offset.shape[0]
    return pl.pallas_call(
        bias_kernel,
        out_shape=jax.ShapeDtypeStruct((heads, length, length), F32),
        name="position_bias",
        cost_estimate=pl.CostEstimate(
            flops=heads * length * length * 4, bytes_accessed=heads * length * length * 4, transcendentals=0
        ),
    )(per_offset)


def dot_n(a, b, precision=None):
    return jnp.dot(a, b, precision=precision, preferred_element_type=F32)


def dot_t(a, b, precision=None):
    return lax.dot_general(a, b, (((1,), (1,)), ((), ())), precision=precision, preferred_element_type=F32)


def t_dot(a, b, precision=None):
    return lax.dot_general(a, b, (((0,), (0,)), ((), ())), precision=precision, preferred_element_type=F32)


def call(kernel, outs, operands, flops, scratch=()):
    moved = sum(o.size * o.dtype.itemsize for o in operands) + sum(
        math.prod(o.shape) * o.dtype.itemsize for o in outs
    )
    return pl.pallas_call(
        kernel,
        out_shape=tuple(outs),
        scratch_shapes=list(scratch),
        cost_estimate=pl.CostEstimate(flops=flops, bytes_accessed=moved, transcendentals=0),
    )(*operands)


def sds(shape, dtype):
    return jax.ShapeDtypeStruct(shape, dtype)


STEP = 256


def unpack_kernel(n_row, index_ref, *refs):
    b_refs, (w_ref, p_ref) = refs[:n_row], refs[n_row:]
    block = b_refs[0].shape[0]
    cols = w_ref.shape[1]
    for k in range(n_row):
        rows = pl.ds(pl.multiple_of((index_ref[0] ^ k) * block, block), block)
        w_ref[rows, :] = b_refs[k][:, :cols]
        p_ref[rows, :] = b_refs[k][:, cols:]


def front_kernel(n_col, heads, normed_ref, w_ref, seg_row_ref, seg_col_ref, bias_ref, perm_ref, *refs):
    qkv_ref, att_ref, probs_ref = refs[:3]
    part_refs = refs[3:]
    qkv_ref[...] = dot_n(normed_ref[...], w_ref[...]).astype(BF)
    length, width = att_ref.shape
    size = width // heads
    seg_row = seg_row_ref[...]

    def body(i, carry):
        rows = pl.ds(pl.multiple_of(i * STEP, STEP), STEP)
        same = seg_col_ref[rows, :] == seg_row
        for h in range(heads):
            q = qkv_ref[rows, h * size : (h + 1) * size]
            k = qkv_ref[:, width + h * size : width + (h + 1) * size]
            v = qkv_ref[:, 2 * width + h * size : 2 * width + (h + 1) * size]
            scores = dot_t(q, k) * size ** (-0.5) + bias_ref[h, rows, :]
            scores = jnp.where(same, scores, NEG)
            top = jnp.max(scores, axis=1, keepdims=True)
            expo = jnp.exp(scores - top)
            probs = expo * (1.0 / jnp.sum(expo, axis=1, keepdims=True))
            probs_ref[h, rows, :] = probs
            att_ref[rows, h * size : (h + 1) * size] = dot_n(probs.astype(BF), v).astype(BF)
        return carry

    lax.fori_loop(0, length // STEP, body, 0)
    own = length // n_col
    for k in range(n_col):
        part_refs[k][...] = dot_n(perm_ref[k * own : (k + 1) * own, :], att_ref[...]).astype(BF)


def router_kernel(n_col, *refs):
    a_refs, p_refs = refs[:n_col], refs[n_col : 2 * n_col]
    tokens_ref, gain_ref, router_ref, picked_ref, slot_ref = refs[2 * n_col : 2 * n_col + 5]
    hidden_ref, probs_ref, gate_ref, send_ref = refs[2 * n_col + 5 :]
    own, width = tokens_ref.shape
    hidden = tokens_ref[...]
    for a_ref, p_ref in zip(a_refs, p_refs):
        hidden = hidden + dot_t(a_ref[...], p_ref[...])
    hidden_ref[...] = hidden
    inverse = lax.rsqrt(jnp.mean(hidden * hidden, axis=1, keepdims=True) + EPS)
    normed = hidden * inverse * gain_ref[...]
    logits = dot_t(normed, router_ref[...], HI)
    expo = jnp.exp(logits - jnp.max(logits, axis=1, keepdims=True))
    probs = expo / jnp.sum(expo, axis=1, keepdims=True)
    probs_ref[...] = probs
    gate = jnp.sum(probs * picked_ref[...], axis=1, keepdims=True)
    gate_ref[...] = gate
    send_ref[:, :width] = dot_n(slot_ref[...], normed.astype(BF)).astype(BF)
    high = gate.astype(BF).astype(F32)
    lane = lax.broadcasted_iota(jnp.int32, (own, 128), 1)
    extra = jnp.where(lane == 0, high, jnp.where(lane == 1, gate - high, 0.0)).astype(BF)
    send_ref[:, width:] = dot_n(slot_ref[...], extra).astype(BF)


def expert_kernel(pairs, *refs):
    row_refs, (w_in_ref, w_out_ref) = refs[:pairs], refs[pairs : pairs + 2]
    mixed_refs, (act_ref, slope_ref) = refs[pairs + 2 : 2 * pairs + 2], refs[2 * pairs + 2 :]
    size, width = mixed_refs[0].shape
    for i in range(pairs):
        part = slice(i * size, (i + 1) * size)
        pre = dot_n(row_refs[i][:, :width], w_in_ref[...])
        bent = jnp.tanh(GELU_C * (pre + GELU_K * pre * pre * pre))
        act = (0.5 * pre * (1.0 + bent)).astype(BF)
        act_ref[part, :] = act
        mixed_refs[i][...] = dot_n(act, w_out_ref[...]).astype(BF)
        slope_ref[part, :] = 0.5 * (1.0 + bent) + 0.5 * pre * (1.0 - bent * bent) * GELU_C * (
            1.0 + 3.0 * GELU_K * pre * pre
        )


def expert_back_kernel(pairs, *refs):
    row_refs, cot_refs = refs[:pairs], refs[pairs : 2 * pairs]
    slope_ref, w_in_ref, w_out_ref = refs[2 * pairs : 2 * pairs + 3]
    back_refs = refs[2 * pairs + 3 : 3 * pairs + 3]
    pre_ref, gated_ref, copy_ref = refs[3 * pairs + 3 :]
    size, width = back_refs[0].shape
    for i in range(pairs):
        part = slice(i * size, (i + 1) * size)
        cot = cot_refs[i][...]
        gate = row_refs[i][:, width : width + 1].astype(F32) + row_refs[i][:, width + 1 : width + 2].astype(F32)
        grad_pre = (gate * dot_t(cot, w_out_ref[...]) * slope_ref[part, :]).astype(BF)
        pre_ref[part, :] = grad_pre
        back_refs[i][...] = dot_t(grad_pre, w_in_ref[...]).astype(BF)
        gated_ref[part, :] = (gate * cot.astype(F32)).astype(BF)
        copy_ref[part, :] = row_refs[i][:, :width]


def pair_kernel(count, *refs):
    total = t_dot(refs[0][...], refs[count][...])
    for k in range(1, count):
        total = total + t_dot(refs[k][...], refs[count + k][...])
    refs[2 * count][...] = total


def token_kernel(
    mixed_ref, back_ref, slot_ref, hidden_ref, tokens_ref, probs_ref, gate_ref, picked_ref, gain_ref,
    router_ref, cot_ref, grad_ref, grad_bf_ref, delta_ref, router_out_ref, mix_ref,
):
    width = hidden_ref.shape[1]
    hidden, gate, cot, gain = hidden_ref[...], gate_ref[...], cot_ref[...], gain_ref[...]
    mixed = t_dot(slot_ref[...], mixed_ref[...])
    back = t_dot(slot_ref[...], back_ref[...])
    delta_ref[...] = (hidden - tokens_ref[...] + gate * mixed).astype(BF)
    grad_gate = jnp.sum(cot * mixed, axis=1, keepdims=True)
    grad_logits = grad_gate * gate * (picked_ref[...] - probs_ref[...])
    inverse = lax.rsqrt(jnp.mean(hidden * hidden, axis=1, keepdims=True) + EPS)
    normed = hidden * inverse * gain
    router_out_ref[...] = t_dot(grad_logits, normed, HI)
    grad_normed = back + dot_n(grad_logits, router_ref[...], HI)
    mix_ref[...] = jnp.sum(grad_normed * hidden * inverse, axis=0, keepdims=True)
    inner = jnp.sum(grad_normed * gain * hidden, axis=1, keepdims=True)
    grad = cot + inverse * gain * grad_normed - hidden * inverse * inverse * inverse * (inner / width)
    grad_ref[...] = grad
    grad_bf_ref[...] = grad.astype(BF)


def back_kernel(n_col, heads, *refs):
    g_refs, a_refs = refs[:n_col], refs[n_col : 2 * n_col]
    proj_ref, perm_ref, qkv_ref, probs_ref, att_ref, normed_ref, onehot_ref = refs[2 * n_col : 2 * n_col + 7]
    wgrad_ref, gq, table_ref = refs[2 * n_col + 7 : 2 * n_col + 10]
    gap, ga, dk, dv, offs = refs[2 * n_col + 10 :]
    length, width = att_ref.shape
    size = width // heads
    scale = size ** (-0.5)
    own = length // n_col
    for k in range(n_col):
        gap[k * own : (k + 1) * own, :] = dot_n(g_refs[k][...], proj_ref[...]).astype(BF)
    ga[...] = dot_n(perm_ref[...], gap[...]).astype(BF)
    dk[...] = jnp.zeros_like(dk)
    dv[...] = jnp.zeros_like(dv)
    offs[...] = jnp.zeros_like(offs)

    def body(i, carry):
        rows = pl.ds(pl.multiple_of(i * STEP, STEP), STEP)
        for h in range(heads):
            cols = slice(h * size, (h + 1) * size)
            q = qkv_ref[rows, cols]
            k = qkv_ref[:, width + h * size : width + (h + 1) * size]
            v = qkv_ref[:, 2 * width + h * size : 2 * width + (h + 1) * size]
            probs = probs_ref[h, rows, :]
            grad_out = ga[rows, cols]
            delta = jnp.sum(
                grad_out.astype(F32) * att_ref[rows, cols].astype(F32), axis=1, keepdims=True
            )
            grad_scores = probs * (dot_t(grad_out, v) - delta)
            grad_bf = grad_scores.astype(BF)
            gq[rows, cols] = (dot_n(grad_bf, k) * scale).astype(BF)
            dk[:, cols] += t_dot(grad_bf, q)
            dv[:, cols] += t_dot(probs.astype(BF), grad_out)
            wide = jnp.concatenate([jnp.zeros_like(grad_scores), grad_scores], axis=1)
            count = STEP // 2
            while count >= 8:
                wide = wide[:count] + pltpu.roll(wide[count:], 2 * length - count, 1)
                count //= 2
            offs[h] += pltpu.roll(wide, 2 * length - 1 - i * STEP, 1)
        return carry

    lax.fori_loop(0, length // STEP, body, 0)
    gq[:, width : 2 * width] = (dk[...] * scale).astype(BF)
    gq[:, 2 * width :] = dv[...].astype(BF)
    wgrad_ref[:, : 3 * width] = t_dot(normed_ref[...], gq[...]).astype(BF)
    total = t_dot(g_refs[0][...], a_refs[0][...])
    for k in range(1, n_col):
        total = total + t_dot(g_refs[k][...], a_refs[k][...])
    wgrad_ref[:, 3 * width :] = total.astype(BF)
    table_ref[...] = jnp.zeros_like(table_ref)
    for h in range(heads):
        rows = offs[h]
        line = rows[0:1]
        for j in range(1, 8):
            line = line + pltpu.roll(rows[j : j + 1], 2 * length - j, 1)
        table_ref[h : h + 1, :] = dot_n(jnp.broadcast_to(line, (8, 2 * length)), onehot_ref[...], HI)[0:1]


def normed_kernel(n_col, gq_ref, perm_ref, w_ref, z_ref, router_ref, mix_ref, table_ref, *refs):
    part_refs, flat_ref = refs[:n_col], refs[n_col]
    own, width = part_refs[0].shape
    experts = router_ref.shape[0]
    total = jnp.zeros((1, width), F32)
    for k in range(n_col):
        rows = slice(k * own, (k + 1) * own)
        moved = dot_n(perm_ref[rows, :], gq_ref[...]).astype(BF)
        part = dot_t(moved, w_ref[...])
        total = total + jnp.sum(part * z_ref[rows, :], axis=0, keepdims=True)
        part_refs[k][...] = part.astype(BF)
    flat_ref[...] = jnp.zeros_like(flat_ref)
    flat_ref[:experts, :] = router_ref[...]
    flat_ref[experts : experts + 1, :] = mix_ref[...]
    flat_ref[experts + 1 : experts + 2, :] = total
    flat_ref[experts + 8 :, :128] = table_ref[...]


def tokens_kernel(mine_ref, came_ref, grad_ref, cot_ref, tokens_ref, inverse_ref, gain_ref, out_ref):
    grad_normed = mine_ref[...].astype(F32) + came_ref[...].astype(F32)
    tokens, inverse, gain = tokens_ref[...], inverse_ref[...], gain_ref[...]
    inner = jnp.sum(grad_normed * gain * tokens, axis=1, keepdims=True)
    delta = (
        (grad_ref[...] - cot_ref[...])
        + inverse * gain * grad_normed
        - tokens * inverse * inverse * inverse * (inner / tokens.shape[1])
    )
    out_ref[...] = delta.astype(BF)


def place_kernel(n_col, *refs):
    b_refs, perm_ref, base_ref, out_ref = refs[:n_col], refs[n_col], refs[n_col + 1], refs[n_col + 2]
    own = b_refs[0].shape[0]
    total = base_ref[...].astype(F32)
    for k in range(n_col):
        total = total + dot_n(perm_ref[:, k * own : (k + 1) * own], b_refs[k][...])
    out_ref[...] = total


def swap(x, axes, count, mask):
    return lax.ppermute(x, axes, [(i, i ^ mask) for i in range(count)])


def bits_of(count):
    return [1 << b for b in range(count.bit_length() - 1)]


def gather_rel(x, axes, count):
    blocks = {0: x}
    for bit in reversed(bits_of(count)):
        new = {}
        for k, v in blocks.items():
            new[k | bit] = swap(v, axes, count, bit)
        blocks.update(new)
    return [blocks[k] for k in range(count)]


def scatter_rel(blocks, axes, count):
    held = dict(enumerate(blocks))
    for bit in bits_of(count):
        got = {k: swap(held[k | bit].astype(BF), axes, count, bit) for k in held if not k & bit}
        held = {k: held[k].astype(F32) + got[k].astype(F32) for k in got}
    return held[0]


def exchange(x, axes):
    return lax.all_to_all(x, axes, split_axis=0, concat_axis=0, tiled=True)


def exchange_rel(blocks, axes, count):
    return [blocks[0]] + [swap(blocks[k], axes, count, k) for k in range(1, count)]


def hold(x, *after):
    return lax.optimization_barrier((x,) + after)[0]


def in_order(blocks, index):
    count = len(blocks)
    if count == 2:
        first = jnp.where(index == 0, blocks[0], blocks[1])
        second = jnp.where(index == 0, blocks[1], blocks[0])
        return jnp.concatenate([first, second], axis=0)
    stacked = jnp.stack(blocks)
    return jnp.concatenate(
        [lax.dynamic_index_in_dim(stacked, index ^ j, 0, keepdims=False) for j in range(count)], axis=0
    )


def body(
    tokens,
    segments,
    routes,
    norm_gain,
    mix_gain,
    qkv_weight,
    proj_weight,
    rel_table,
    router_weight,
    expert_in,
    expert_out,
    cotangent,
):
    n_dp, n_row, n_col = lax.axis_size("dp"), lax.axis_size("row"), lax.axis_size("col")
    experts = n_dp * n_row
    dp, row, col = lax.axis_index("dp"), lax.axis_index("row"), lax.axis_index("col")
    count, width = tokens.shape
    length = segments.shape[1]
    heads = rel_table.shape[1]
    local = proj_weight.shape[0]
    block = width // n_row
    own = count // n_col
    slots = 2 * count // experts // n_col
    total_slots = experts * slots
    w_in, w_out = expert_in[0], expert_out[0]

    packed = jnp.concatenate([qkv_weight.reshape(block, 3 * local), proj_weight.T], axis=1)
    packed_rel = gather_rel(packed, "row", n_row)
    weight, proj_local = pl.pallas_call(
        partial(unpack_kernel, n_row),
        out_shape=(sds((width, 3 * local), BF), sds((width, local), BF)),
        in_specs=[pl.BlockSpec(memory_space=pltpu.SMEM)] + [pl.BlockSpec(memory_space=pltpu.VMEM)] * n_row,
        name="unpack",
        cost_estimate=pl.CostEstimate(flops=0, bytes_accessed=16 * width * local, transcendentals=0),
    )(row.reshape(1).astype(jnp.int32), *packed_rel)

    chosen = routes[:, 0]
    expert_ids = jnp.arange(experts, dtype=jnp.int32)
    hits = (expert_ids[:, None] == chosen[None, :]).astype(F32)
    place = jnp.arange(count, dtype=jnp.int32)
    before = (place[:, None] < place[None, :]).astype(BF)
    earlier = dot_n(hits.astype(BF), before)
    totals = jnp.sum(hits, axis=1)
    starts = jnp.sum(
        jnp.where(expert_ids[None, :] < expert_ids[:, None], totals[None, :], 0.0), axis=1
    )
    start = jnp.sum(hits * starts[:, None], axis=0).astype(jnp.int32)
    rank = jnp.sum(hits * earlier, axis=0).astype(jnp.int32)
    spot = start + rank
    owner, inner = spot % n_col, spot // n_col
    dest = (owner ^ col) * own + inner
    perm = (place[:, None] == dest[None, :]).astype(BF)
    perm_t = (dest[:, None] == place[None, :]).astype(BF)
    perm_own = perm[:own]
    local_rank = inner - (start + n_col - 1 - col) // n_col
    slot = jnp.where(owner == col, chosen * slots + local_rank, -1)
    slot_ids = jnp.arange(total_slots, dtype=jnp.int32)
    slot_of_token = (slot_ids[:, None] == slot[None, :]).astype(BF)
    slot_of_own = dot_t(slot_of_token, perm_own).astype(BF)
    picked = dot_t(perm_own, hits.astype(BF))

    inputs = tokens.astype(F32)
    inverse = lax.rsqrt(jnp.mean(inputs * inputs, axis=1, keepdims=True) + EPS)
    normed_bf = (inputs * inverse * norm_gain).astype(BF)
    tokens_perm = dot_n(perm, tokens)
    inverse_perm = lax.rsqrt(jnp.mean(tokens_perm * tokens_perm, axis=1, keepdims=True) + EPS)
    tokens_own, inverse_own = tokens_perm[:own], inverse_perm[:own]

    onehot = offset_onehot(length)
    per_offset = dot_n(rel_table.T, onehot[:, :BUCKETS].T, HI)
    bias = position_bias(per_offset, length)

    cot_slots = dot_n(slot_of_token, cotangent.astype(BF)).astype(BF)
    cot_slots = hold(cot_slots, packed_rel[n_row // 2])
    cot_came = exchange(cot_slots.reshape(experts, slots, width), DR).reshape(total_slots, width)
    cot_blocks = gather_rel(cot_came, "col", n_col)
    proj_blocks = gather_rel(proj_local, "col", n_col)
    seg_row, seg_col = segments.reshape(1, length), segments.reshape(length, 1)
    qkv_rows, attended, probs, *att_parts = call(
        partial(front_kernel, n_col, heads),
        [sds((length, 3 * local), BF), sds((length, local), BF), sds((heads, length, length), F32)]
        + [sds((own, local), BF)] * n_col,
        [normed_bf, weight, seg_row, seg_col, bias, perm],
        2 * length * local * (3 * width + 3 * length),
    )
    att_own = exchange_rel(att_parts, "col", n_col)

    router_t = router_weight.T
    mix_row, gain_row = mix_gain.reshape(1, width), norm_gain.reshape(1, width)
    hidden, router_probs, gate, token_slots = call(
        partial(router_kernel, n_col),
        [sds((own, width), F32), sds((own, experts), F32), sds((own, 1), F32), sds((total_slots, width + 128), BF)],
        [*att_own, *proj_blocks, tokens_own, mix_row, router_t, picked, slot_of_own],
        2 * own * width * (width + total_slots),
    )

    token_slots = hold(token_slots, cot_came)
    token_came = exchange(token_slots.reshape(experts, slots, width + 128), DR)
    token_blocks = gather_rel(token_came.reshape(total_slots, width + 128), "col", n_col)
    pairs = 2
    row = sds((total_slots, width), BF)
    twice = sds((pairs * total_slots, width), BF)
    work = 4 * pairs * total_slots * width * width
    mixed_parts, back_parts, acts, slopes, behind = [], [], [], [], []
    for k in range(0, n_col, pairs):
        *mixed, act, slope = call(
            partial(expert_kernel, pairs), [row] * pairs + [twice, sds(twice.shape, F32)],
            [*token_blocks[k : k + pairs], w_in, w_out], work,
        )
        mixed_parts += mixed
        acts.append(act)
        slopes.append(slope)
    for k in range(0, n_col, pairs):
        *back, pre, gated, rows = call(
            partial(expert_back_kernel, pairs), [row] * pairs + [twice] * 3,
            [*token_blocks[k : k + pairs], *cot_blocks[k : k + pairs], slopes[k // pairs], w_in, w_out],
            work,
        )
        back_parts += back
        behind.append((pre, gated, rows))

    def to_home(parts):
        summed = scatter_rel(parts, "col", n_col).astype(BF)
        return exchange(summed.reshape(experts, slots, width), DR).reshape(total_slots, width)

    mixed_came = to_home(mixed_parts)
    back_came = to_home(back_parts)
    work = 2 * n_col * total_slots * width * width
    grad_in_local, = call(
        partial(pair_kernel, len(behind)), [sds((width, width), F32)],
        [r for _, _, r in behind] + [p for p, _, _ in behind], work,
    )
    grad_out_local, = call(
        partial(pair_kernel, len(behind)), [sds((width, width), F32)],
        acts + [g for _, g, _ in behind], work,
    )
    mixed_came, grad_in_local, grad_out_local = lax.optimization_barrier(
        (mixed_came, grad_in_local, grad_out_local)
    )

    cot_own = dot_n(perm_own.astype(F32), cotangent, HI)
    z_perm = hold(tokens_perm, mixed_parts[0]) * inverse_perm
    mixed_came, z_perm = lax.optimization_barrier((mixed_came, z_perm))

    grad_hidden, grad_hidden_bf, out_delta, router_local, mix_local = call(
        token_kernel,
        [sds((own, width), F32), sds((own, width), BF), sds((own, width), BF), sds((experts, width), F32),
         sds((1, width), F32)],
        [mixed_came, back_came, slot_of_own, hidden, tokens_own, router_probs, gate, picked, mix_row,
         router_t, cot_own],
        4 * own * width * total_slots,
    )
    grad_blocks = gather_rel(grad_hidden_bf, "col", n_col)
    out_blocks = gather_rel(hold(out_delta, *grad_blocks), "col", n_col)

    wgrad, grad_qkv, table_local = call(
        partial(back_kernel, n_col, heads),
        [sds((width, 4 * local), BF), sds((length, 3 * local), BF), sds((8, 128), F32)],
        [*grad_blocks, *att_parts, proj_local, perm_t, qkv_rows, probs, attended, normed_bf, onehot],
        2 * length * local * (5 * width + 5 * length),
        [pltpu.VMEM((length, local), BF), pltpu.VMEM((length, local), BF),
         pltpu.VMEM((length, local), F32), pltpu.VMEM((length, local), F32), pltpu.VMEM((heads, 8, 2 * length), F32)],
    )
    wgrad_came = exchange(wgrad.reshape(experts, block // n_dp, 4 * local), ("row", "dp"))
    *normed_parts, flat = call(
        partial(normed_kernel, n_col),
        [sds((own, width), BF)] * n_col + [sds((experts + 16, width), F32)],
        [grad_qkv, perm, weight, z_perm, router_local, mix_local, table_local],
        2 * length * local * 3 * (width + length),
    )
    held = dict(enumerate(normed_parts))
    for bit in bits_of(n_col)[:-1]:
        got = {k: swap(held[k | bit], "col", n_col, bit) for k in held if not k & bit}
        held = {k: (held[k].astype(F32) + got[k].astype(F32)).astype(BF) for k in got}
    last = n_col // 2
    normed_came = swap(held[last], "col", n_col, last)
    first_sum = held[0]
    tokens_delta, = call(
        tokens_kernel, [sds((own, width), BF)],
        [first_sum, normed_came, grad_hidden, cot_own, tokens_own, inverse_own, gain_row],
        own * width * 12,
    )
    delta_blocks = gather_rel(tokens_delta, "col", n_col)
    output, = call(
        partial(place_kernel, n_col), [sds((count, width), F32)], [*out_blocks, perm_t, tokens],
        2 * count * count * width,
    )
    grad_tokens, = call(
        partial(place_kernel, n_col), [sds((count, width), F32)], [*delta_blocks, perm_t, cotangent],
        2 * count * count * width,
    )
    summed = jnp.sum(wgrad_came.astype(F32), axis=0).astype(BF)
    summed = in_order(gather_rel(summed, "dp", n_dp), dp).astype(F32)
    grad_qkv_weight = summed[:, : 3 * local].reshape(block, 3, local)
    grad_proj = summed[:, 3 * local :].T

    packed = experts + 8
    most, table = flat[:packed], flat[packed:]
    most = hold(most, first_sum)
    for bit in bits_of(n_col):
        most = most + swap(most, "col", n_col, bit)
    flat = hold(jnp.concatenate([most, table], axis=0), wgrad_came)
    for bit in bits_of(experts):
        flat = flat + swap(flat, DR, experts, bit)
    grad_table = flat[packed : packed + heads, :BUCKETS].T
    grad_router = flat[:experts].T
    grad_mix, grad_norm = flat[experts], flat[experts + 1]
    return (
        output,
        grad_tokens,
        grad_qkv_weight,
        grad_proj,
        grad_table,
        grad_norm,
        grad_mix,
        grad_router,
        grad_in_local[None],
        grad_out_local[None],
    )


def solution(mesh):
    placed = (
        P(("dp", "row"), None),
        P(("dp", "row"), None),
        P(("dp", "row"), None),
        P(),
        P(),
        P("row", None, "col"),
        P("col", "row"),
        P(None, "col"),
        P(),
        P(("dp", "row"), None, "col"),
        P(("dp", "row"), "col", None),
        P(("dp", "row"), None),
    )
    return jax.shard_map(
        body,
        mesh=mesh,
        in_specs=placed,
        out_specs=(
            P(("dp", "row"), None),
            P(("dp", "row"), None),
            P("row", None, "col"),
            P("col", "row"),
            P(None, "col"),
            P(),
            P(),
            P(),
            P(("dp", "row"), None, "col"),
            P(("dp", "row"), "col", None),
        ),
        check_vma=False,
    )
```

```python
from functools import partial
import math

import jax
import jax.numpy as jnp
from jax import lax
from jax.experimental import pallas as pl
from jax.experimental.pallas import tpu as pltpu
from jax.sharding import PartitionSpec as P

BUCKETS = 32
MAX_DIST = 128
EPS = 1e-06
NEG = -1e30
GELU_C = 0.7978845608028654
GELU_K = 0.044715
BF = jnp.bfloat16
F32 = jnp.float32
HI = lax.Precision.HIGHEST
DR = ("dp", "row")


def bucket_edges():
    half_count = BUCKETS // 2
    exact_count = half_count // 2
    edge_list = []
    for target in range(1, half_count):
        if target < exact_count:
            edge_list.append(target)
        else:
            for distance in range(exact_count, MAX_DIST + 1):
                reached = exact_count + int(
                    math.log(distance / exact_count)
                    / math.log(MAX_DIST / exact_count)
                    * (half_count - exact_count)
                )
                if min(reached, half_count - 1) >= target:
                    edge_list.append(distance)
                    break
    return edge_list


def offset_onehot(length):
    offsets = jnp.arange(2 * length, dtype=jnp.int32) - (length - 1)
    magnitude = jnp.abs(offsets)
    ids = jnp.where(offsets > 0, BUCKETS // 2, 0)
    for border in bucket_edges():
        ids = ids + (magnitude >= border).astype(jnp.int32)
    ids = jnp.where(offsets >= length, -1, ids)
    return (ids[:, None] == jnp.arange(128, dtype=jnp.int32)[None, :]).astype(F32)


def bias_kernel(off_ref, out_ref):
    heads, length, _ = out_ref.shape
    for h in range(heads):
        rows = jnp.broadcast_to(off_ref[h : h + 1, :], (length, 2 * length))
        skewed = pltpu.roll(rows, 1, 1, stride=1, stride_axis=0)
        out_ref[h] = skewed[:, length:]


def position_bias(per_offset, length):
    heads = per_offset.shape[0]
    return pl.pallas_call(
        bias_kernel,
        out_shape=jax.ShapeDtypeStruct((heads, length, length), F32),
        name="position_bias",
        cost_estimate=pl.CostEstimate(
            flops=heads * length * length * 4, bytes_accessed=heads * length * length * 4, transcendentals=0
        ),
    )(per_offset)


def dot_n(a, b, precision=None):
    return jnp.dot(a, b, precision=precision, preferred_element_type=F32)


def dot_t(a, b, precision=None):
    return lax.dot_general(a, b, (((1,), (1,)), ((), ())), precision=precision, preferred_element_type=F32)


def t_dot(a, b, precision=None):
    return lax.dot_general(a, b, (((0,), (0,)), ((), ())), precision=precision, preferred_element_type=F32)


def call(kernel, outs, operands, flops, scratch=(), scalars=()):
    moved = sum(o.size * o.dtype.itemsize for o in operands) + sum(
        math.prod(o.shape) * o.dtype.itemsize for o in outs
    )
    return pl.pallas_call(
        kernel,
        out_shape=tuple(outs),
        in_specs=[pl.BlockSpec(memory_space=pltpu.SMEM)] * len(scalars)
        + [pl.BlockSpec(memory_space=pltpu.VMEM)] * len(operands),
        scratch_shapes=list(scratch),
        cost_estimate=pl.CostEstimate(flops=flops, bytes_accessed=moved, transcendentals=0),
    )(*scalars, *operands)


def chunk_rows(me_ref, k, size):
    return pl.ds(pl.multiple_of((me_ref[0] ^ k) * size, size), size)


def sds(shape, dtype):
    return jax.ShapeDtypeStruct(shape, dtype)


STEP = 256


def unpack_kernel(n_row, index_ref, *refs):
    b_refs, (w_ref, p_ref) = refs[:n_row], refs[n_row:]
    block = b_refs[0].shape[0]
    cols = w_ref.shape[1]
    for k in range(n_row):
        rows = pl.ds(pl.multiple_of((index_ref[0] ^ k) * block, block), block)
        w_ref[rows, :] = b_refs[k][:, :cols]
        p_ref[rows, :] = b_refs[k][:, cols:]


def front_kernel(n_col, heads, normed_ref, w_ref, seg_row_ref, seg_col_ref, bias_ref, perm_ref, *refs):
    qkv_ref, att_ref, probs_ref = refs[:3]
    part_refs = refs[3:]
    qkv_ref[...] = dot_n(normed_ref[...], w_ref[...]).astype(BF)
    length, width = att_ref.shape
    size = width // heads
    seg_row = seg_row_ref[...]

    def body(i, carry):
        rows = pl.ds(pl.multiple_of(i * STEP, STEP), STEP)
        same = seg_col_ref[rows, :] == seg_row
        for h in range(heads):
            q = qkv_ref[rows, h * size : (h + 1) * size]
            k = qkv_ref[:, width + h * size : width + (h + 1) * size]
            v = qkv_ref[:, 2 * width + h * size : 2 * width + (h + 1) * size]
            scores = dot_t(q, k) * size ** (-0.5) + bias_ref[h, rows, :]
            scores = jnp.where(same, scores, NEG)
            top = jnp.max(scores, axis=1, keepdims=True)
            expo = jnp.exp(scores - top)
            probs = (expo * (1.0 / jnp.sum(expo, axis=1, keepdims=True))).astype(BF)
            probs_ref[h, rows, :] = probs
            att_ref[rows, h * size : (h + 1) * size] = dot_n(probs, v).astype(BF)
        return carry

    lax.fori_loop(0, length // STEP, body, 0)
    own = length // n_col
    for k in range(n_col):
        part_refs[k][...] = dot_n(perm_ref[k * own : (k + 1) * own, :], att_ref[...]).astype(BF)


def router_kernel(n_col, *refs):
    a_refs, p_refs = refs[:n_col], refs[n_col : 2 * n_col]
    tokens_ref, gain_ref, router_ref, picked_ref, slot_ref = refs[2 * n_col : 2 * n_col + 5]
    hidden_ref, probs_ref, gate_ref, send_ref = refs[2 * n_col + 5 :]
    own, width = tokens_ref.shape
    hidden = tokens_ref[...]
    for a_ref, p_ref in zip(a_refs, p_refs):
        hidden = hidden + dot_t(a_ref[...], p_ref[...])
    hidden_ref[...] = hidden
    inverse = lax.rsqrt(jnp.mean(hidden * hidden, axis=1, keepdims=True) + EPS)
    normed = hidden * inverse * gain_ref[0:1, :]
    logits = dot_t(normed, router_ref[...], HI)
    expo = jnp.exp(logits - jnp.max(logits, axis=1, keepdims=True))
    probs = expo / jnp.sum(expo, axis=1, keepdims=True)
    probs_ref[...] = probs
    gate = jnp.sum(probs * picked_ref[...], axis=1, keepdims=True)
    gate_ref[...] = gate
    send_ref[:, :width] = dot_n(slot_ref[...], normed.astype(BF)).astype(BF)
    high = gate.astype(BF).astype(F32)
    lane = lax.broadcasted_iota(jnp.int32, (own, 128), 1)
    extra = jnp.where(lane == 0, high, jnp.where(lane == 1, gate - high, 0.0)).astype(BF)
    send_ref[:, width:] = dot_n(slot_ref[...], extra).astype(BF)


def split_kernel(me_ref, a_ref, b_ref, c_ref, *refs):
    size = refs[0].shape[0]
    for k, part_ref in enumerate(refs):
        rows = chunk_rows(me_ref, k, size)
        total = a_ref[rows, :].astype(F32) + b_ref[rows, :].astype(F32) + c_ref[rows, :].astype(F32)
        part_ref[...] = total.astype(BF)


def expert_kernel(pairs, *refs):
    row_refs, (w_in_ref, w_out_ref) = refs[:pairs], refs[pairs : pairs + 2]
    mixed_refs, (act_ref, slope_ref) = refs[pairs + 2 : 2 * pairs + 2], refs[2 * pairs + 2 :]
    size, width = mixed_refs[0].shape
    for i in range(pairs):
        part = slice(i * size, (i + 1) * size)
        pre = dot_n(row_refs[i][:, :width], w_in_ref[...])
        bent = jnp.tanh(GELU_C * (pre + GELU_K * pre * pre * pre))
        act = (0.5 * pre * (1.0 + bent)).astype(BF)
        act_ref[part, :] = act
        mixed_refs[i][...] = dot_n(act, w_out_ref[...]).astype(BF)
        slope_ref[part, :] = 0.5 * (1.0 + bent) + 0.5 * pre * (1.0 - bent * bent) * GELU_C * (
            1.0 + 3.0 * GELU_K * pre * pre
        )


def expert_back_kernel(pairs, *refs):
    row_refs, cot_refs = refs[:pairs], refs[pairs : 2 * pairs]
    slope_ref, w_in_ref, w_out_ref = refs[2 * pairs : 2 * pairs + 3]
    back_refs = refs[2 * pairs + 3 : 3 * pairs + 3]
    pre_ref, gated_ref, copy_ref = refs[3 * pairs + 3 :]
    size, width = back_refs[0].shape
    for i in range(pairs):
        part = slice(i * size, (i + 1) * size)
        cot = cot_refs[i][...]
        gate = row_refs[i][:, width : width + 1].astype(F32) + row_refs[i][:, width + 1 : width + 2].astype(F32)
        grad_pre = (gate * dot_t(cot, w_out_ref[...]) * slope_ref[part, :]).astype(BF)
        pre_ref[part, :] = grad_pre
        back_refs[i][...] = dot_t(grad_pre, w_in_ref[...]).astype(BF)
        gated_ref[part, :] = (gate * cot.astype(F32)).astype(BF)
        copy_ref[part, :] = row_refs[i][:, :width]


def pair_kernel(count, *refs):
    total = t_dot(refs[0][...], refs[count][...])
    for k in range(1, count):
        total = total + t_dot(refs[k][...], refs[count + k][...])
    refs[2 * count][...] = total


def mixed_kernel(came_ref, slot_ref, hidden_ref, tokens_ref, gate_ref, mixed_ref, delta_ref):
    mixed = t_dot(slot_ref[...], came_ref[...])
    mixed_ref[...] = mixed
    delta_ref[...] = (hidden_ref[...] - tokens_ref[...] + gate_ref[...] * mixed).astype(BF)


def token_kernel(chunks, me_ref, mixed_ref, *refs):
    back_refs = refs[:chunks]
    (slot_ref, hidden_ref, probs_ref, gate_ref, picked_ref, gain_ref, router_ref, cot_ref,
     grad_ref, grad_bf_ref, router_out_ref, mix_ref, all_ref) = refs[chunks:]
    size = back_refs[0].shape[0]
    for k in range(chunks):
        all_ref[chunk_rows(me_ref, k, size), :] = back_refs[k][...]
    width = hidden_ref.shape[1]
    hidden, gate, cot, gain = hidden_ref[...], gate_ref[...], cot_ref[...], gain_ref[0:1, :]
    mixed = mixed_ref[...]
    back = t_dot(slot_ref[...], all_ref[...])
    grad_gate = jnp.sum(cot * mixed, axis=1, keepdims=True)
    grad_logits = grad_gate * gate * (picked_ref[...] - probs_ref[...])
    inverse = lax.rsqrt(jnp.mean(hidden * hidden, axis=1, keepdims=True) + EPS)
    normed = hidden * inverse * gain
    router_out_ref[...] = t_dot(grad_logits, normed, HI)
    grad_normed = back + dot_n(grad_logits, router_ref[...], HI)
    mix_ref[...] = jnp.sum(grad_normed * hidden * inverse, axis=0, keepdims=True)
    inner = jnp.sum(grad_normed * gain * hidden, axis=1, keepdims=True)
    grad = cot + inverse * gain * grad_normed - hidden * inverse * inverse * inverse * (inner / width)
    grad_ref[...] = grad
    grad_bf_ref[...] = grad.astype(BF)


def back_kernel(n_col, heads, *refs):
    g_refs, a_refs = refs[:n_col], refs[n_col : 2 * n_col]
    proj_ref, perm_ref, qkv_ref, probs_ref, att_ref, normed_ref, onehot_ref = refs[2 * n_col : 2 * n_col + 7]
    wgrad_ref, gq, table_ref = refs[2 * n_col + 7 : 2 * n_col + 10]
    gap, ga, dk, dv, offs = refs[2 * n_col + 10 :]
    length, width = att_ref.shape
    size = width // heads
    scale = size ** (-0.5)
    own = length // n_col
    for k in range(n_col):
        gap[k * own : (k + 1) * own, :] = dot_n(g_refs[k][...], proj_ref[...]).astype(BF)
    ga[...] = dot_n(perm_ref[...], gap[...]).astype(BF)
    dk[...] = jnp.zeros_like(dk)
    dv[...] = jnp.zeros_like(dv)
    offs[...] = jnp.zeros_like(offs)

    def body(i, carry):
        rows = pl.ds(pl.multiple_of(i * STEP, STEP), STEP)
        for h in range(heads):
            cols = slice(h * size, (h + 1) * size)
            q = qkv_ref[rows, cols]
            k = qkv_ref[:, width + h * size : width + (h + 1) * size]
            v = qkv_ref[:, 2 * width + h * size : 2 * width + (h + 1) * size]
            probs = probs_ref[h, rows, :]
            grad_out = ga[rows, cols]
            delta = jnp.sum(
                grad_out.astype(F32) * att_ref[rows, cols].astype(F32), axis=1, keepdims=True
            )
            grad_scores = probs.astype(F32) * (dot_t(grad_out, v) - delta)
            grad_bf = grad_scores.astype(BF)
            gq[rows, cols] = (dot_n(grad_bf, k) * scale).astype(BF)
            dk[:, cols] += t_dot(grad_bf, q)
            dv[:, cols] += t_dot(probs, grad_out)
            wide = jnp.concatenate([jnp.zeros_like(grad_scores), grad_scores], axis=1)
            count = STEP // 2
            while count >= 8:
                wide = wide[:count] + pltpu.roll(wide[count:], 2 * length - count, 1)
                count //= 2
            offs[h] += pltpu.roll(wide, 2 * length - 1 - i * STEP, 1)
        return carry

    lax.fori_loop(0, length // STEP, body, 0)
    gq[:, width : 2 * width] = (dk[...] * scale).astype(BF)
    gq[:, 2 * width :] = dv[...].astype(BF)
    wgrad_ref[:, : 3 * width] = t_dot(normed_ref[...], gq[...]).astype(BF)
    total = t_dot(g_refs[0][...], a_refs[0][...])
    for k in range(1, n_col):
        total = total + t_dot(g_refs[k][...], a_refs[k][...])
    wgrad_ref[:, 3 * width :] = total.astype(BF)
    table_ref[...] = jnp.zeros_like(table_ref)
    for h in range(heads):
        rows = offs[h]
        line = rows[0:1]
        for j in range(1, 8):
            line = line + pltpu.roll(rows[j : j + 1], 2 * length - j, 1)
        table_ref[h : h + 1, :] = dot_n(jnp.broadcast_to(line, (8, 2 * length)), onehot_ref[...], HI)[0:1]


def normed_kernel(n_col, col_ref, gq_ref, perm_ref, w_ref, z_ref, router_ref, mix_ref, table_ref, *refs):
    part_refs, flat_ref = refs[:n_col], refs[n_col]
    own, width = part_refs[0].shape
    experts = router_ref.shape[0]
    total = jnp.zeros((1, width), F32)
    for k in range(n_col):
        rows = slice(k * own, (k + 1) * own)
        moved = dot_n(perm_ref[rows, :], gq_ref[...]).astype(BF)
        part = dot_t(moved, w_ref[...])
        total = total + jnp.sum(part * z_ref[rows, :], axis=0, keepdims=True)
        part_refs[k][...] = part.astype(BF)
    flat_ref[...] = jnp.zeros_like(flat_ref)
    flat_ref[:experts, :] = router_ref[...]
    flat_ref[experts : experts + 1, :] = mix_ref[...]
    flat_ref[experts + 1 : experts + 2, :] = total
    flat_ref[experts + 8 :, pl.ds(pl.multiple_of(col_ref[0] * 128, 128), 128)] = table_ref[...]


def tokens_kernel(a_ref, b_ref, c_ref, grad_ref, cot_ref, tokens_ref, gain_ref, out_ref):
    grad_normed = a_ref[...].astype(F32) + b_ref[...].astype(F32) + c_ref[...].astype(F32)
    tokens, gain = tokens_ref[...], gain_ref[1:2, :]
    inverse = lax.rsqrt(jnp.mean(tokens * tokens, axis=1, keepdims=True) + EPS)
    inner = jnp.sum(grad_normed * gain * tokens, axis=1, keepdims=True)
    delta = (
        (grad_ref[...] - cot_ref[...])
        + inverse * gain * grad_normed
        - tokens * inverse * inverse * inverse * (inner / tokens.shape[1])
    )
    out_ref[...] = delta.astype(BF)


def place_kernel(n_col, *refs):
    b_refs, perm_ref, base_ref, out_ref = refs[:n_col], refs[n_col], refs[n_col + 1], refs[n_col + 2]
    own = b_refs[0].shape[0]
    total = base_ref[...].astype(F32)
    for k in range(n_col):
        total = total + dot_n(perm_ref[:, k * own : (k + 1) * own], b_refs[k][...])
    out_ref[...] = total


def place_rows(blocks, perm_t, base):
    count, width = base.shape
    return call(
        partial(place_kernel, len(blocks)), [sds(base.shape, F32)], [*blocks, perm_t, base],
        2 * count * count * width,
    )[0]


def swap(x, axes, count, mask):
    return lax.ppermute(x, axes, [(i, i ^ mask) for i in range(count)])


def bits_of(count):
    return [1 << b for b in range(count.bit_length() - 1)]


def gather_rel(x, axes, count):
    blocks = {0: x}
    for bit in reversed(bits_of(count)):
        new = {}
        for k, v in blocks.items():
            new[k | bit] = swap(v, axes, count, bit)
        blocks.update(new)
    return [blocks[k] for k in range(count)]


def sum_all(x, axes, count):
    terms = [x]
    for k in range(1, count):
        terms.append(swap(x, axes, count, k))
    while len(terms) > 1:
        terms = [terms[i] + terms[i + 1] for i in range(0, len(terms), 2)]
    return terms[0]


def exchange(x, axes):
    return lax.all_to_all(x, axes, split_axis=0, concat_axis=0, tiled=True)


def exchange_rel(blocks, axes, count):
    return [blocks[0]] + [swap(blocks[k], axes, count, k) for k in range(1, count)]


def hold(x, *after):
    return lax.optimization_barrier((x,) + after)[0]


def in_order(blocks, index):
    count = len(blocks)
    if count == 2:
        first = jnp.where(index == 0, blocks[0], blocks[1])
        second = jnp.where(index == 0, blocks[1], blocks[0])
        return jnp.concatenate([first, second], axis=0)
    stacked = jnp.stack(blocks)
    return jnp.concatenate(
        [lax.dynamic_index_in_dim(stacked, index ^ j, 0, keepdims=False) for j in range(count)], axis=0
    )


def body(
    tokens,
    segments,
    routes,
    norm_gain,
    mix_gain,
    qkv_weight,
    proj_weight,
    rel_table,
    router_weight,
    expert_in,
    expert_out,
    cotangent,
):
    n_dp, n_row, n_col = lax.axis_size("dp"), lax.axis_size("row"), lax.axis_size("col")
    experts = n_dp * n_row
    dp, row, col = lax.axis_index("dp"), lax.axis_index("row"), lax.axis_index("col")
    me = dp * n_row + row
    count, width = tokens.shape
    length = segments.shape[1]
    heads = rel_table.shape[1]
    local = proj_weight.shape[0]
    block = width // n_row
    own = count // n_col
    slots = 2 * count // experts // n_col
    total_slots = experts * slots
    w_in, w_out = expert_in[0], expert_out[0]

    packed = jnp.concatenate([qkv_weight.reshape(block, 3 * local), proj_weight.T], axis=1)
    packed_rel = gather_rel(packed, "row", n_row)
    weight, proj_local = pl.pallas_call(
        partial(unpack_kernel, n_row),
        out_shape=(sds((width, 3 * local), BF), sds((width, local), BF)),
        in_specs=[pl.BlockSpec(memory_space=pltpu.SMEM)] + [pl.BlockSpec(memory_space=pltpu.VMEM)] * n_row,
        name="unpack",
        cost_estimate=pl.CostEstimate(flops=0, bytes_accessed=16 * width * local, transcendentals=0),
    )(row.reshape(1).astype(jnp.int32), *packed_rel)

    chosen = routes[:, 0]
    expert_ids = jnp.arange(experts, dtype=jnp.int32)
    hits = (expert_ids[:, None] == chosen[None, :]).astype(F32)
    place = jnp.arange(count, dtype=jnp.int32)
    before = (place[:, None] < place[None, :]).astype(BF)
    earlier = dot_n(hits.astype(BF), before)
    totals = jnp.sum(hits, axis=1)
    starts = jnp.sum(
        jnp.where(expert_ids[None, :] < expert_ids[:, None], totals[None, :], 0.0), axis=1
    )
    start = jnp.sum(hits * starts[:, None], axis=0).astype(jnp.int32)
    rank = jnp.sum(hits * earlier, axis=0).astype(jnp.int32)
    spot = start + rank
    owner, inner = spot % n_col, spot // n_col
    dest = (owner ^ col) * own + inner
    perm = (place[:, None] == dest[None, :]).astype(BF)
    perm_t = (dest[:, None] == place[None, :]).astype(BF)
    perm_own = perm[:own]
    local_rank = inner - (start + n_col - 1 - col) // n_col
    slot = jnp.where(owner == col, chosen * slots + local_rank, -1)
    slot_ids = jnp.arange(total_slots, dtype=jnp.int32)
    slot_of_token = (slot_ids[:, None] == slot[None, :]).astype(BF)
    slot_of_own = dot_t(slot_of_token, perm_own).astype(BF)
    picked = dot_t(perm_own, hits.astype(BF))

    inputs = tokens.astype(F32)
    inverse = lax.rsqrt(jnp.mean(inputs * inputs, axis=1, keepdims=True) + EPS)
    normed_bf = (inputs * inverse * norm_gain).astype(BF)
    tokens_perm = dot_n(perm, tokens)
    inverse_perm = lax.rsqrt(jnp.mean(tokens_perm * tokens_perm, axis=1, keepdims=True) + EPS)
    tokens_own = tokens_perm[:own]

    gains = jnp.stack([mix_gain, norm_gain])
    seg_row = segments.reshape(1, length)
    seg_col = jnp.sum(jnp.where(place[:, None] == place[None, :], seg_row, 0), axis=1, keepdims=True)

    onehot = offset_onehot(length)
    per_offset = dot_n(rel_table.T, onehot[:, :BUCKETS].T, HI)
    bias = position_bias(per_offset, length)

    cot_slots = dot_n(slot_of_token, cotangent.astype(BF)).astype(BF)
    cot_slots = hold(cot_slots, packed_rel[n_row // 2])
    cot_came = exchange(cot_slots.reshape(experts, slots, width), DR).reshape(total_slots, width)
    cot_blocks = gather_rel(cot_came, "col", n_col)
    proj_blocks = gather_rel(proj_local, "col", n_col)
    qkv_rows, attended, probs, *att_parts = call(
        partial(front_kernel, n_col, heads),
        [sds((length, 3 * local), BF), sds((length, local), BF), sds((heads, length, length), BF)]
        + [sds((own, local), BF)] * n_col,
        [normed_bf, weight, seg_row, seg_col, bias, perm],
        2 * length * local * (3 * width + 3 * length),
    )
    att_own = exchange_rel(att_parts, "col", n_col)

    router_t = router_weight.T
    cot_own = dot_n(perm_own.astype(F32), cotangent, HI)
    z_perm = tokens_perm * inverse_perm
    chunks = experts if experts <= 8 else 1
    chunk = total_slots // chunks
    wide = width + 128
    here = me.reshape(1).astype(jnp.int32)
    zero = jnp.zeros((1,), jnp.int32)
    where = here if chunks > 1 else zero
    hidden, router_probs, gate, token_slots = call(
        partial(router_kernel, n_col),
        [sds((own, width), F32), sds((own, experts), F32), sds((own, 1), F32), sds((total_slots, wide), BF)],
        [*att_own, *proj_blocks, tokens_own, gains, router_t, picked, slot_of_own],
        2 * own * width * (width + total_slots),
    )

    def trade(parts):
        if chunks == 1:
            return [exchange(parts[0].reshape(experts, slots, -1), DR).reshape(total_slots, -1)]
        out = [parts[0]]
        for k in range(1, chunks):
            out.append(swap(parts[k], DR, experts, k))
        return out

    token_slots = hold(token_slots, cot_came)
    token_came = exchange(token_slots.reshape(experts, slots, wide), DR).reshape(total_slots, wide)
    token_blocks = gather_rel(token_came, "col", n_col)
    pairs = 2
    row = sds((total_slots, width), BF)
    twice = sds((pairs * total_slots, width), BF)
    work = 4 * pairs * total_slots * width * width
    mixed_parts, back_parts, acts, slopes, behind = [], [], [], [], []
    for k in range(0, n_col, pairs):
        *mixed, act, slope = call(
            partial(expert_kernel, pairs), [row] * pairs + [twice, sds(twice.shape, F32)],
            [*token_blocks[k : k + pairs], w_in, w_out], work,
        )
        mixed_parts += mixed
        acts.append(act)
        slopes.append(slope)
    for k in range(0, n_col, pairs):
        *back, pre, gated, rows = call(
            partial(expert_back_kernel, pairs), [row] * pairs + [twice] * 3,
            [*token_blocks[k : k + pairs], *cot_blocks[k : k + pairs], slopes[k // pairs], w_in, w_out],
            work,
        )
        back_parts += back
        behind.append((pre, gated, rows))

    def to_col(parts):
        held = {k: [p] for k, p in enumerate(parts)}
        for bit in bits_of(n_col)[:-1]:
            ready = {k: v[0] if len(v) == 1 else sum(t.astype(F32) for t in v).astype(BF) for k, v in held.items()}
            held = {
                k: [ready[k], swap(ready[k | bit], "col", n_col, bit)] for k in sorted(held) if not k & bit
            }
        return held[0], sum(t.astype(F32) for t in held[n_col // 2]).astype(BF)

    mine, other = to_col(mixed_parts)
    came = swap(other, "col", n_col, n_col // 2)
    mixed_sum = sum(t.astype(F32) for t in (*mine, came)).astype(BF)
    mixed_came = exchange(mixed_sum.reshape(experts, slots, width), DR).reshape(total_slots, width)
    mine, other = to_col(back_parts)
    came = swap(other, "col", n_col, n_col // 2)
    back_split = call(split_kernel, [sds((chunk, width), BF)] * chunks, [*mine, came], 0, scalars=[where])
    back_came = trade(back_split)
    work = 2 * n_col * total_slots * width * width
    grad_in_local, = call(
        partial(pair_kernel, len(behind)), [sds((width, width), F32)],
        [r for _, _, r in behind] + [p for p, _, _ in behind], work,
    )
    grad_out_local, = call(
        partial(pair_kernel, len(behind)), [sds((width, width), F32)],
        acts + [g for _, g, _ in behind], work,
    )

    mixed, out_delta = call(
        mixed_kernel, [sds((own, width), F32), sds((own, width), BF)],
        [mixed_came, slot_of_own, hidden, tokens_own, gate], 2 * own * width * total_slots,
    )
    out_blocks = gather_rel(out_delta, "col", n_col)
    output = place_rows(out_blocks, perm_t, tokens)
    grad_hidden, grad_hidden_bf, router_local, mix_local = call(
        partial(token_kernel, chunks),
        [sds((own, width), F32), sds((own, width), BF), sds((experts, width), F32), sds((1, width), F32)],
        [mixed, *back_came, slot_of_own, hidden, router_probs, gate, picked, gains, router_t, cot_own],
        2 * own * width * total_slots, [pltpu.VMEM((total_slots, width), BF)], [where],
    )
    grad_blocks = gather_rel(grad_hidden_bf, "col", n_col)

    wgrad, grad_qkv, table_local = call(
        partial(back_kernel, n_col, heads),
        [sds((width, 4 * local), BF), sds((length, 3 * local), BF), sds((8, 128), F32)],
        [*grad_blocks, *att_parts, proj_local, perm_t, qkv_rows, probs, attended, normed_bf, onehot],
        2 * length * local * (5 * width + 5 * length),
        [pltpu.VMEM((length, local), BF), pltpu.VMEM((length, local), BF),
         pltpu.VMEM((length, local), F32), pltpu.VMEM((length, local), F32), pltpu.VMEM((heads, 8, 2 * length), F32)],
    )
    wgrad_came = exchange(wgrad.reshape(experts, block // n_dp, 4 * local), ("row", "dp"))
    *normed_parts, flat = call(
        partial(normed_kernel, n_col),
        [sds((own, width), BF)] * n_col + [sds((experts + 16, width), F32)],
        [grad_qkv, perm, weight, z_perm, router_local, mix_local, table_local],
        2 * length * local * 3 * (width + length), scalars=[col.reshape(1).astype(jnp.int32)],
    )
    mine, other = to_col(normed_parts)
    normed_came = swap(other, "col", n_col, n_col // 2)
    tokens_delta, = call(
        tokens_kernel, [sds((own, width), BF)],
        [*mine, normed_came, grad_hidden, cot_own, tokens_own, gains],
        own * width * 12,
    )
    delta_blocks = gather_rel(tokens_delta, "col", n_col)
    grad_tokens = place_rows(delta_blocks, perm_t, cotangent)
    summed = jnp.sum(wgrad_came.astype(F32), axis=0).astype(BF)
    summed = in_order(gather_rel(summed, "dp", n_dp), dp).astype(F32)
    grad_qkv_weight = summed[:, : 3 * local].reshape(block, 3, local)
    grad_proj = summed[:, 3 * local :].T

    packed = experts + 8
    flat = sum_all(hold(flat, other), "col", n_col)
    flat = sum_all(flat, "row", n_row)
    flat = sum_all(flat, "dp", n_dp)
    grad_table = lax.dynamic_slice(flat, (packed, col * 128), (heads, BUCKETS)).T
    grad_router = flat[:experts].T
    grad_mix, grad_norm = flat[experts], flat[experts + 1]
    return (
        output,
        grad_tokens,
        grad_qkv_weight,
        grad_proj,
        grad_table,
        grad_norm,
        grad_mix,
        grad_router,
        grad_in_local[None],
        grad_out_local[None],
    )


def solution(mesh):
    placed = (
        P(("dp", "row"), None),
        P(("dp", "row"), None),
        P(("dp", "row"), None),
        P(),
        P(),
        P("row", None, "col"),
        P("col", "row"),
        P(None, "col"),
        P(),
        P(("dp", "row"), None, "col"),
        P(("dp", "row"), "col", None),
        P(("dp", "row"), None),
    )
    return jax.shard_map(
        body,
        mesh=mesh,
        in_specs=placed,
        out_specs=(
            P(("dp", "row"), None),
            P(("dp", "row"), None),
            P("row", None, "col"),
            P("col", "row"),
            P(None, "col"),
            P(),
            P(),
            P(),
            P(("dp", "row"), None, "col"),
            P(("dp", "row"), "col", None),
        ),
        check_vma=False,
    )
```

```python
from functools import partial
import math

import jax
import jax.numpy as jnp
from jax import lax
from jax.experimental import pallas as pl
from jax.experimental.pallas import tpu as pltpu
from jax.sharding import PartitionSpec as P

BUCKETS = 32
MAX_DIST = 128
EPS = 1e-06
NEG = -1e30
GELU_C = 0.7978845608028654
GELU_K = 0.044715
BF = jnp.bfloat16
F32 = jnp.float32
HI = lax.Precision.HIGHEST
DR = ("dp", "row")


def bucket_edges():
    half_count = BUCKETS // 2
    exact_count = half_count // 2
    edge_list = []
    for target in range(1, half_count):
        if target < exact_count:
            edge_list.append(target)
        else:
            for distance in range(exact_count, MAX_DIST + 1):
                reached = exact_count + int(
                    math.log(distance / exact_count)
                    / math.log(MAX_DIST / exact_count)
                    * (half_count - exact_count)
                )
                if min(reached, half_count - 1) >= target:
                    edge_list.append(distance)
                    break
    return edge_list


def offset_onehot(length):
    offsets = jnp.arange(2 * length, dtype=jnp.int32) - (length - 1)
    magnitude = jnp.abs(offsets)
    ids = jnp.where(offsets > 0, BUCKETS // 2, 0)
    for border in bucket_edges():
        ids = ids + (magnitude >= border).astype(jnp.int32)
    ids = jnp.where(offsets >= length, -1, ids)
    return (ids[:, None] == jnp.arange(128, dtype=jnp.int32)[None, :]).astype(F32)


def bias_kernel(off_ref, out_ref):
    heads, length, _ = out_ref.shape
    for h in range(heads):
        rows = jnp.broadcast_to(off_ref[h : h + 1, :], (length, 2 * length))
        skewed = pltpu.roll(rows, 1, 1, stride=1, stride_axis=0)
        out_ref[h] = skewed[:, length:]


def position_bias(per_offset, length):
    heads = per_offset.shape[0]
    return pl.pallas_call(
        bias_kernel,
        out_shape=jax.ShapeDtypeStruct((heads, length, length), F32),
        name="position_bias",
        cost_estimate=pl.CostEstimate(
            flops=heads * length * length * 4, bytes_accessed=heads * length * length * 4, transcendentals=0
        ),
    )(per_offset)


def dot_n(a, b, precision=None):
    return jnp.dot(a, b, precision=precision, preferred_element_type=F32)


def dot_t(a, b, precision=None):
    return lax.dot_general(a, b, (((1,), (1,)), ((), ())), precision=precision, preferred_element_type=F32)


def t_dot(a, b, precision=None):
    return lax.dot_general(a, b, (((0,), (0,)), ((), ())), precision=precision, preferred_element_type=F32)


def call(kernel, outs, operands, flops, scratch=(), scalars=()):
    moved = sum(o.size * o.dtype.itemsize for o in operands) + sum(
        math.prod(o.shape) * o.dtype.itemsize for o in outs
    )
    return pl.pallas_call(
        kernel,
        out_shape=tuple(outs),
        in_specs=[pl.BlockSpec(memory_space=pltpu.SMEM)] * len(scalars)
        + [pl.BlockSpec(memory_space=pltpu.VMEM)] * len(operands),
        scratch_shapes=list(scratch),
        cost_estimate=pl.CostEstimate(flops=flops, bytes_accessed=moved, transcendentals=0),
    )(*scalars, *operands)


def chunk_rows(me_ref, k, size):
    return pl.ds(pl.multiple_of((me_ref[0] ^ k) * size, size), size)


def sds(shape, dtype):
    return jax.ShapeDtypeStruct(shape, dtype)


STEP = 512


def unpack_kernel(n_row, index_ref, *refs):
    b_refs, (w_ref, p_ref) = refs[:n_row], refs[n_row:]
    block = b_refs[0].shape[0]
    cols = w_ref.shape[1]
    for k in range(n_row):
        rows = pl.ds(pl.multiple_of((index_ref[0] ^ k) * block, block), block)
        w_ref[rows, :] = b_refs[k][:, :cols]
        p_ref[rows, :] = b_refs[k][:, cols:]


def front_kernel(n_col, heads, normed_ref, w_ref, seg_row_ref, seg_col_ref, bias_ref, perm_ref, *refs):
    qkv_ref, att_ref, probs_ref = refs[:3]
    part_refs = refs[3:]
    qkv_ref[...] = dot_n(normed_ref[...], w_ref[...]).astype(BF)
    length, width = att_ref.shape
    size = width // heads
    seg_row = seg_row_ref[...]

    def body(i, carry):
        rows = pl.ds(pl.multiple_of(i * STEP, STEP), STEP)
        same = seg_col_ref[rows, :] == seg_row
        for h in range(heads):
            q = qkv_ref[rows, h * size : (h + 1) * size]
            k = qkv_ref[:, width + h * size : width + (h + 1) * size]
            v = qkv_ref[:, 2 * width + h * size : 2 * width + (h + 1) * size]
            scores = dot_t(q, k) * size ** (-0.5) + bias_ref[h, rows, :]
            scores = jnp.where(same, scores, NEG)
            top = jnp.max(scores, axis=1, keepdims=True)
            expo = jnp.exp(scores - top)
            probs = (expo * (1.0 / jnp.sum(expo, axis=1, keepdims=True))).astype(BF)
            probs_ref[h, rows, :] = probs
            att_ref[rows, h * size : (h + 1) * size] = dot_n(probs, v).astype(BF)
        return carry

    lax.fori_loop(0, length // STEP, body, 0)
    own = length // n_col
    for k in range(n_col):
        part_refs[k][...] = dot_n(perm_ref[k * own : (k + 1) * own, :], att_ref[...]).astype(BF)


def router_kernel(n_col, *refs):
    a_refs, p_refs = refs[:n_col], refs[n_col : 2 * n_col]
    tokens_ref, gain_ref, router_ref, picked_ref, slot_ref = refs[2 * n_col : 2 * n_col + 5]
    hidden_ref, probs_ref, gate_ref, send_ref = refs[2 * n_col + 5 :]
    own, width = tokens_ref.shape
    hidden = tokens_ref[...]
    for a_ref, p_ref in zip(a_refs, p_refs):
        hidden = hidden + dot_t(a_ref[...], p_ref[...])
    hidden_ref[...] = hidden
    inverse = lax.rsqrt(jnp.mean(hidden * hidden, axis=1, keepdims=True) + EPS)
    normed = hidden * inverse * gain_ref[0:1, :]
    logits = dot_t(normed, router_ref[...], HI)
    expo = jnp.exp(logits - jnp.max(logits, axis=1, keepdims=True))
    probs = expo / jnp.sum(expo, axis=1, keepdims=True)
    probs_ref[...] = probs
    gate = jnp.sum(probs * picked_ref[...], axis=1, keepdims=True)
    gate_ref[...] = gate
    send_ref[:, :width] = dot_n(slot_ref[...], normed.astype(BF)).astype(BF)
    high = gate.astype(BF).astype(F32)
    lane = lax.broadcasted_iota(jnp.int32, (own, 128), 1)
    extra = jnp.where(lane == 0, high, jnp.where(lane == 1, gate - high, 0.0)).astype(BF)
    send_ref[:, width:] = dot_n(slot_ref[...], extra).astype(BF)


def split_kernel(me_ref, a_ref, b_ref, c_ref, *refs):
    size = refs[0].shape[0]
    for k, part_ref in enumerate(refs):
        rows = chunk_rows(me_ref, k, size)
        total = a_ref[rows, :].astype(F32) + b_ref[rows, :].astype(F32) + c_ref[rows, :].astype(F32)
        part_ref[...] = total.astype(BF)


def expert_kernel(pairs, *refs):
    row_refs, (w_in_ref, w_out_ref) = refs[:pairs], refs[pairs : pairs + 2]
    mixed_refs, (act_ref, slope_ref) = refs[pairs + 2 : 2 * pairs + 2], refs[2 * pairs + 2 :]
    size, width = mixed_refs[0].shape
    for i in range(pairs):
        part = slice(i * size, (i + 1) * size)
        pre = dot_n(row_refs[i][:, :width], w_in_ref[...])
        bent = jnp.tanh(GELU_C * (pre + GELU_K * pre * pre * pre))
        act = (0.5 * pre * (1.0 + bent)).astype(BF)
        act_ref[part, :] = act
        mixed_refs[i][...] = dot_n(act, w_out_ref[...]).astype(BF)
        slope_ref[part, :] = 0.5 * (1.0 + bent) + 0.5 * pre * (1.0 - bent * bent) * GELU_C * (
            1.0 + 3.0 * GELU_K * pre * pre
        )


def expert_back_kernel(pairs, *refs):
    row_refs, cot_refs = refs[:pairs], refs[pairs : 2 * pairs]
    slope_ref, w_in_ref, w_out_ref = refs[2 * pairs : 2 * pairs + 3]
    back_refs = refs[2 * pairs + 3 : 3 * pairs + 3]
    pre_ref, gated_ref, copy_ref = refs[3 * pairs + 3 :]
    size, width = back_refs[0].shape
    for i in range(pairs):
        part = slice(i * size, (i + 1) * size)
        cot = cot_refs[i][...]
        gate = row_refs[i][:, width : width + 1].astype(F32) + row_refs[i][:, width + 1 : width + 2].astype(F32)
        grad_pre = (gate * dot_t(cot, w_out_ref[...]) * slope_ref[part, :]).astype(BF)
        pre_ref[part, :] = grad_pre
        back_refs[i][...] = dot_t(grad_pre, w_in_ref[...]).astype(BF)
        gated_ref[part, :] = (gate * cot.astype(F32)).astype(BF)
        copy_ref[part, :] = row_refs[i][:, :width]


def pair_kernel(count, *refs):
    total = t_dot(refs[0][...], refs[count][...])
    for k in range(1, count):
        total = total + t_dot(refs[k][...], refs[count + k][...])
    refs[2 * count][...] = total


def mixed_kernel(came_ref, slot_ref, hidden_ref, tokens_ref, gate_ref, mixed_ref, delta_ref):
    mixed = t_dot(slot_ref[...], came_ref[...])
    mixed_ref[...] = mixed
    delta_ref[...] = (hidden_ref[...] - tokens_ref[...] + gate_ref[...] * mixed).astype(BF)


def token_kernel(chunks, me_ref, mixed_ref, *refs):
    back_refs = refs[:chunks]
    (slot_ref, hidden_ref, probs_ref, gate_ref, picked_ref, gain_ref, router_ref, cot_ref,
     grad_ref, grad_bf_ref, router_out_ref, mix_ref, all_ref) = refs[chunks:]
    size = back_refs[0].shape[0]
    for k in range(chunks):
        all_ref[chunk_rows(me_ref, k, size), :] = back_refs[k][...]
    width = hidden_ref.shape[1]
    hidden, gate, cot, gain = hidden_ref[...], gate_ref[...], cot_ref[...], gain_ref[0:1, :]
    mixed = mixed_ref[...]
    back = t_dot(slot_ref[...], all_ref[...])
    grad_gate = jnp.sum(cot * mixed, axis=1, keepdims=True)
    grad_logits = grad_gate * gate * (picked_ref[...] - probs_ref[...])
    inverse = lax.rsqrt(jnp.mean(hidden * hidden, axis=1, keepdims=True) + EPS)
    normed = hidden * inverse * gain
    router_out_ref[...] = t_dot(grad_logits, normed, HI)
    grad_normed = back + dot_n(grad_logits, router_ref[...], HI)
    mix_ref[...] = jnp.sum(grad_normed * hidden * inverse, axis=0, keepdims=True)
    inner = jnp.sum(grad_normed * gain * hidden, axis=1, keepdims=True)
    grad = cot + inverse * gain * grad_normed - hidden * inverse * inverse * inverse * (inner / width)
    grad_ref[...] = grad
    grad_bf_ref[...] = grad.astype(BF)


def back_kernel(n_col, heads, *refs):
    g_refs, a_refs = refs[:n_col], refs[n_col : 2 * n_col]
    proj_ref, perm_ref, qkv_ref, probs_ref, att_ref, normed_ref, onehot_ref = refs[2 * n_col : 2 * n_col + 7]
    wgrad_ref, gq, table_ref = refs[2 * n_col + 7 : 2 * n_col + 10]
    gap, ga, dk, dv, offs = refs[2 * n_col + 10 :]
    length, width = att_ref.shape
    size = width // heads
    scale = size ** (-0.5)
    own = length // n_col
    for k in range(n_col):
        gap[k * own : (k + 1) * own, :] = dot_n(g_refs[k][...], proj_ref[...]).astype(BF)
    ga[...] = dot_n(perm_ref[...], gap[...]).astype(BF)
    dk[...] = jnp.zeros_like(dk)
    dv[...] = jnp.zeros_like(dv)
    offs[...] = jnp.zeros_like(offs)

    def body(i, carry):
        rows = pl.ds(pl.multiple_of(i * STEP, STEP), STEP)
        for h in range(heads):
            cols = slice(h * size, (h + 1) * size)
            q = qkv_ref[rows, cols]
            k = qkv_ref[:, width + h * size : width + (h + 1) * size]
            v = qkv_ref[:, 2 * width + h * size : 2 * width + (h + 1) * size]
            probs = probs_ref[h, rows, :]
            grad_out = ga[rows, cols]
            delta = jnp.sum(
                grad_out.astype(F32) * att_ref[rows, cols].astype(F32), axis=1, keepdims=True
            )
            grad_scores = probs.astype(F32) * (dot_t(grad_out, v) - delta)
            grad_bf = grad_scores.astype(BF)
            gq[rows, cols] = (dot_n(grad_bf, k) * scale).astype(BF)
            dk[:, cols] += t_dot(grad_bf, q)
            dv[:, cols] += t_dot(probs, grad_out)
            wide = jnp.concatenate([jnp.zeros_like(grad_scores), grad_scores], axis=1)
            count = STEP // 2
            while count >= 8:
                wide = wide[:count] + pltpu.roll(wide[count:], 2 * length - count, 1)
                count //= 2
            offs[h] += pltpu.roll(wide, 2 * length - 1 - i * STEP, 1)
        return carry

    lax.fori_loop(0, length // STEP, body, 0)
    gq[:, width : 2 * width] = (dk[...] * scale).astype(BF)
    gq[:, 2 * width :] = dv[...].astype(BF)
    wgrad_ref[:, : 3 * width] = t_dot(normed_ref[...], gq[...]).astype(BF)
    total = t_dot(g_refs[0][...], a_refs[0][...])
    for k in range(1, n_col):
        total = total + t_dot(g_refs[k][...], a_refs[k][...])
    wgrad_ref[:, 3 * width :] = total.astype(BF)
    table_ref[...] = jnp.zeros_like(table_ref)
    for h in range(heads):
        rows = offs[h]
        line = rows[0:1]
        for j in range(1, 8):
            line = line + pltpu.roll(rows[j : j + 1], 2 * length - j, 1)
        table_ref[h : h + 1, :] = dot_n(jnp.broadcast_to(line, (8, 2 * length)), onehot_ref[...], HI)[0:1]


def normed_kernel(n_col, col_ref, gq_ref, perm_ref, w_ref, z_ref, router_ref, mix_ref, table_ref, *refs):
    part_refs, flat_ref = refs[:n_col], refs[n_col]
    own, width = part_refs[0].shape
    experts = router_ref.shape[0]
    total = jnp.zeros((1, width), F32)
    for k in range(n_col):
        rows = slice(k * own, (k + 1) * own)
        moved = dot_n(perm_ref[rows, :], gq_ref[...]).astype(BF)
        part = dot_t(moved, w_ref[...])
        total = total + jnp.sum(part * z_ref[rows, :], axis=0, keepdims=True)
        part_refs[k][...] = part.astype(BF)
    flat_ref[...] = jnp.zeros_like(flat_ref)
    flat_ref[:experts, :] = router_ref[...]
    flat_ref[experts : experts + 1, :] = mix_ref[...]
    flat_ref[experts + 1 : experts + 2, :] = total
    flat_ref[experts + 2 :, pl.ds(pl.multiple_of(col_ref[0] * 128, 128), 128)] = table_ref[:6, :]


def tokens_kernel(a_ref, b_ref, c_ref, grad_ref, cot_ref, tokens_ref, gain_ref, out_ref):
    grad_normed = a_ref[...].astype(F32) + b_ref[...].astype(F32) + c_ref[...].astype(F32)
    tokens, gain = tokens_ref[...], gain_ref[1:2, :]
    inverse = lax.rsqrt(jnp.mean(tokens * tokens, axis=1, keepdims=True) + EPS)
    inner = jnp.sum(grad_normed * gain * tokens, axis=1, keepdims=True)
    delta = (
        (grad_ref[...] - cot_ref[...])
        + inverse * gain * grad_normed
        - tokens * inverse * inverse * inverse * (inner / tokens.shape[1])
    )
    out_ref[...] = delta.astype(BF)


def place_kernel(n_col, *refs):
    b_refs, perm_ref, base_ref, out_ref = refs[:n_col], refs[n_col], refs[n_col + 1], refs[n_col + 2]
    own = b_refs[0].shape[0]
    total = base_ref[...].astype(F32)
    for k in range(n_col):
        total = total + dot_n(perm_ref[:, k * own : (k + 1) * own], b_refs[k][...])
    out_ref[...] = total


def place_rows(blocks, perm_t, base):
    count, width = base.shape
    return call(
        partial(place_kernel, len(blocks)), [sds(base.shape, F32)], [*blocks, perm_t, base],
        2 * count * count * width,
    )[0]


def swap(x, axes, count, mask):
    return lax.ppermute(x, axes, [(i, i ^ mask) for i in range(count)])


def bits_of(count):
    return [1 << b for b in range(count.bit_length() - 1)]


def gather_rel(x, axes, count):
    blocks = {0: x}
    for bit in reversed(bits_of(count)):
        new = {}
        for k, v in blocks.items():
            new[k | bit] = swap(v, axes, count, bit)
        blocks.update(new)
    return [blocks[k] for k in range(count)]


def sum_all(x, axes, count):
    terms = [x]
    for k in range(1, count):
        terms.append(swap(x, axes, count, k))
    while len(terms) > 1:
        terms = [terms[i] + terms[i + 1] for i in range(0, len(terms), 2)]
    return terms[0]


def exchange(x, axes):
    return lax.all_to_all(x, axes, split_axis=0, concat_axis=0, tiled=True)


def exchange_rel(blocks, axes, count):
    return [blocks[0]] + [swap(blocks[k], axes, count, k) for k in range(1, count)]


def hold(x, *after):
    return lax.optimization_barrier((x,) + after)[0]


def in_order(blocks, index):
    count = len(blocks)
    if count == 2:
        first = jnp.where(index == 0, blocks[0], blocks[1])
        second = jnp.where(index == 0, blocks[1], blocks[0])
        return jnp.concatenate([first, second], axis=0)
    stacked = jnp.stack(blocks)
    return jnp.concatenate(
        [lax.dynamic_index_in_dim(stacked, index ^ j, 0, keepdims=False) for j in range(count)], axis=0
    )


def body(
    tokens,
    segments,
    routes,
    norm_gain,
    mix_gain,
    qkv_weight,
    proj_weight,
    rel_table,
    router_weight,
    expert_in,
    expert_out,
    cotangent,
):
    n_dp, n_row, n_col = lax.axis_size("dp"), lax.axis_size("row"), lax.axis_size("col")
    experts = n_dp * n_row
    dp, row, col = lax.axis_index("dp"), lax.axis_index("row"), lax.axis_index("col")
    me = dp * n_row + row
    count, width = tokens.shape
    length = segments.shape[1]
    heads = rel_table.shape[1]
    local = proj_weight.shape[0]
    block = width // n_row
    own = count // n_col
    slots = 2 * count // experts // n_col
    total_slots = experts * slots
    w_in, w_out = expert_in[0], expert_out[0]

    packed = jnp.concatenate([qkv_weight.reshape(block, 3 * local), proj_weight.T], axis=1)
    packed_rel = gather_rel(packed, "row", n_row)
    weight, proj_local = pl.pallas_call(
        partial(unpack_kernel, n_row),
        out_shape=(sds((width, 3 * local), BF), sds((width, local), BF)),
        in_specs=[pl.BlockSpec(memory_space=pltpu.SMEM)] + [pl.BlockSpec(memory_space=pltpu.VMEM)] * n_row,
        name="unpack",
        cost_estimate=pl.CostEstimate(flops=0, bytes_accessed=16 * width * local, transcendentals=0),
    )(row.reshape(1).astype(jnp.int32), *packed_rel)

    chosen = routes[:, 0]
    expert_ids = jnp.arange(experts, dtype=jnp.int32)
    hits = (expert_ids[:, None] == chosen[None, :]).astype(F32)
    place = jnp.arange(count, dtype=jnp.int32)
    before = (place[:, None] < place[None, :]).astype(BF)
    earlier = dot_n(hits.astype(BF), before)
    totals = jnp.sum(hits, axis=1)
    starts = jnp.sum(
        jnp.where(expert_ids[None, :] < expert_ids[:, None], totals[None, :], 0.0), axis=1
    )
    start = jnp.sum(hits * starts[:, None], axis=0).astype(jnp.int32)
    rank = jnp.sum(hits * earlier, axis=0).astype(jnp.int32)
    spot = start + rank
    owner, inner = spot % n_col, spot // n_col
    dest = (owner ^ col) * own + inner
    perm = (place[:, None] == dest[None, :]).astype(BF)
    perm_t = (dest[:, None] == place[None, :]).astype(BF)
    perm_own = perm[:own]
    local_rank = inner - (start + n_col - 1 - col) // n_col
    slot = jnp.where(owner == col, chosen * slots + local_rank, -1)
    slot_ids = jnp.arange(total_slots, dtype=jnp.int32)
    slot_of_token = (slot_ids[:, None] == slot[None, :]).astype(BF)

    inputs = tokens.astype(F32)
    inverse = lax.rsqrt(jnp.mean(inputs * inputs, axis=1, keepdims=True) + EPS)
    normed_bf = (inputs * inverse * norm_gain).astype(BF)
    tokens_perm = dot_n(perm, tokens)
    inverse_perm = lax.rsqrt(jnp.mean(tokens_perm * tokens_perm, axis=1, keepdims=True) + EPS)
    tokens_own = tokens_perm[:own]

    seg_row = segments.reshape(1, length)
    seg_col = jnp.sum(jnp.where(place[:, None] == place[None, :], seg_row, 0), axis=1, keepdims=True)

    onehot = offset_onehot(length)
    per_offset = dot_n(rel_table.T, onehot[:, :BUCKETS].T, HI)
    bias = position_bias(per_offset, length)

    cot_slots = dot_n(slot_of_token, cotangent.astype(BF)).astype(BF)
    cot_slots = hold(cot_slots, packed_rel[n_row // 2])
    cot_came = exchange(cot_slots.reshape(experts, slots, width), DR).reshape(total_slots, width)
    cot_blocks = gather_rel(cot_came, "col", n_col)
    slot_of_own = dot_t(slot_of_token, perm_own).astype(BF)
    picked = dot_t(perm_own, hits.astype(BF))
    gains = jnp.stack([mix_gain, norm_gain])

    proj_blocks = gather_rel(proj_local, "col", n_col)
    qkv_rows, attended, probs, *att_parts = call(
        partial(front_kernel, n_col, heads),
        [sds((length, 3 * local), BF), sds((length, local), BF), sds((heads, length, length), BF)]
        + [sds((own, local), BF)] * n_col,
        [normed_bf, weight, seg_row, seg_col, bias, perm],
        2 * length * local * (3 * width + 3 * length),
    )
    att_own = exchange_rel(att_parts, "col", n_col)

    router_t = router_weight.T
    cot_own = dot_n(perm_own.astype(F32), cotangent, HI)
    z_perm = tokens_perm * inverse_perm
    chunks = experts if experts <= 8 else 1
    chunk = total_slots // chunks
    wide = width + 128
    here = me.reshape(1).astype(jnp.int32)
    zero = jnp.zeros((1,), jnp.int32)
    where = here if chunks > 1 else zero
    hidden, router_probs, gate, token_slots = call(
        partial(router_kernel, n_col),
        [sds((own, width), F32), sds((own, experts), F32), sds((own, 1), F32), sds((total_slots, wide), BF)],
        [*att_own, *proj_blocks, tokens_own, gains, router_t, picked, slot_of_own],
        2 * own * width * (width + total_slots),
    )

    def trade(parts):
        if chunks == 1:
            return [exchange(parts[0].reshape(experts, slots, -1), DR).reshape(total_slots, -1)]
        out = [parts[0]]
        for k in range(1, chunks):
            out.append(swap(parts[k], DR, experts, k))
        return out

    token_slots = hold(token_slots, cot_came)
    token_came = exchange(token_slots.reshape(experts, slots, wide), DR).reshape(total_slots, wide)
    token_blocks = gather_rel(token_came, "col", n_col)
    pairs = 2
    row = sds((total_slots, width), BF)
    twice = sds((pairs * total_slots, width), BF)
    work = 4 * pairs * total_slots * width * width
    mixed_parts, back_parts, acts, slopes, behind = [], [], [], [], []
    for k in range(0, n_col, pairs):
        *mixed, act, slope = call(
            partial(expert_kernel, pairs), [row] * pairs + [twice, sds(twice.shape, F32)],
            [*token_blocks[k : k + pairs], w_in, w_out], work,
        )
        mixed_parts += mixed
        acts.append(act)
        slopes.append(slope)
    for k in range(0, n_col, pairs):
        *back, pre, gated, rows = call(
            partial(expert_back_kernel, pairs), [row] * pairs + [twice] * 3,
            [*token_blocks[k : k + pairs], *cot_blocks[k : k + pairs], slopes[k // pairs], w_in, w_out],
            work,
        )
        back_parts += back
        behind.append((pre, gated, rows))

    def to_col(parts):
        held = {k: [p] for k, p in enumerate(parts)}
        for bit in bits_of(n_col)[:-1]:
            ready = {k: v[0] if len(v) == 1 else sum(t.astype(F32) for t in v).astype(BF) for k, v in held.items()}
            held = {
                k: [ready[k], swap(ready[k | bit], "col", n_col, bit)] for k in sorted(held) if not k & bit
            }
        return held[0], sum(t.astype(F32) for t in held[n_col // 2]).astype(BF)

    mine, other = to_col(mixed_parts)
    came = swap(other, "col", n_col, n_col // 2)
    mixed_sum = sum(t.astype(F32) for t in (*mine, came)).astype(BF)
    mixed_came = exchange(mixed_sum.reshape(experts, slots, width), DR).reshape(total_slots, width)
    mine, other = to_col(back_parts)
    came = swap(other, "col", n_col, n_col // 2)
    back_split = call(split_kernel, [sds((chunk, width), BF)] * chunks, [*mine, came], 0, scalars=[where])
    back_came = trade(back_split)
    work = 2 * n_col * total_slots * width * width
    grad_in_local, = call(
        partial(pair_kernel, len(behind)), [sds((width, width), F32)],
        [r for _, _, r in behind] + [p for p, _, _ in behind], work,
    )
    grad_out_local, = call(
        partial(pair_kernel, len(behind)), [sds((width, width), F32)],
        acts + [g for _, g, _ in behind], work,
    )

    mixed, out_delta = call(
        mixed_kernel, [sds((own, width), F32), sds((own, width), BF)],
        [mixed_came, slot_of_own, hidden, tokens_own, gate], 2 * own * width * total_slots,
    )
    out_blocks = gather_rel(out_delta, "col", n_col)
    output = place_rows(out_blocks, perm_t, tokens)
    grad_hidden, grad_hidden_bf, router_local, mix_local = call(
        partial(token_kernel, chunks),
        [sds((own, width), F32), sds((own, width), BF), sds((experts, width), F32), sds((1, width), F32)],
        [mixed, *back_came, slot_of_own, hidden, router_probs, gate, picked, gains, router_t, cot_own],
        2 * own * width * total_slots, [pltpu.VMEM((total_slots, width), BF)], [where],
    )
    grad_blocks = gather_rel(grad_hidden_bf, "col", n_col)

    wgrad, grad_qkv, table_local = call(
        partial(back_kernel, n_col, heads),
        [sds((width, 4 * local), BF), sds((length, 3 * local), BF), sds((8, 128), F32)],
        [*grad_blocks, *att_parts, proj_local, perm_t, qkv_rows, probs, attended, normed_bf, onehot],
        2 * length * local * (5 * width + 5 * length),
        [pltpu.VMEM((length, local), BF), pltpu.VMEM((length, local), BF),
         pltpu.VMEM((length, local), F32), pltpu.VMEM((length, local), F32), pltpu.VMEM((heads, 8, 2 * length), F32)],
    )
    wgrad_came = exchange(wgrad.reshape(experts, block // n_dp, 4 * local), ("row", "dp"))
    *normed_parts, flat = call(
        partial(normed_kernel, n_col),
        [sds((own, width), BF)] * n_col + [sds((experts + 8, width), F32)],
        [grad_qkv, perm, weight, z_perm, router_local, mix_local, table_local],
        2 * length * local * 3 * (width + length), scalars=[col.reshape(1).astype(jnp.int32)],
    )
    mine, other = to_col(normed_parts)
    normed_came = swap(other, "col", n_col, n_col // 2)
    tokens_delta, = call(
        tokens_kernel, [sds((own, width), BF)],
        [*mine, normed_came, grad_hidden, cot_own, tokens_own, gains],
        own * width * 12,
    )
    delta_blocks = gather_rel(tokens_delta, "col", n_col)
    grad_tokens = place_rows(delta_blocks, perm_t, cotangent)
    summed = jnp.sum(wgrad_came.astype(F32), axis=0).astype(BF)
    summed = in_order(gather_rel(summed, "dp", n_dp), dp).astype(F32)
    grad_qkv_weight = summed[:, : 3 * local].reshape(block, 3, local)
    grad_proj = summed[:, 3 * local :].T

    packed = experts + 2
    flat = sum_all(hold(flat, other), "col", n_col)
    flat = sum_all(flat, "row", n_row)
    flat = sum_all(flat, "dp", n_dp)
    grad_table = lax.dynamic_slice(flat, (packed, col * 128), (heads, BUCKETS)).T
    grad_router = flat[:experts].T
    grad_mix, grad_norm = flat[experts], flat[experts + 1]
    return (
        output,
        grad_tokens,
        grad_qkv_weight,
        grad_proj,
        grad_table,
        grad_norm,
        grad_mix,
        grad_router,
        grad_in_local[None],
        grad_out_local[None],
    )


def solution(mesh):
    placed = (
        P(("dp", "row"), None),
        P(("dp", "row"), None),
        P(("dp", "row"), None),
        P(),
        P(),
        P("row", None, "col"),
        P("col", "row"),
        P(None, "col"),
        P(),
        P(("dp", "row"), None, "col"),
        P(("dp", "row"), "col", None),
        P(("dp", "row"), None),
    )
    return jax.shard_map(
        body,
        mesh=mesh,
        in_specs=placed,
        out_specs=(
            P(("dp", "row"), None),
            P(("dp", "row"), None),
            P("row", None, "col"),
            P("col", "row"),
            P(None, "col"),
            P(),
            P(),
            P(),
            P(("dp", "row"), None, "col"),
            P(("dp", "row"), "col", None),
        ),
        check_vma=False,
    )
```
